32 devices in a mesh: pipe: 4 (over z), tensor: 4 (over x, core), dp: 2 (over y).
Axes of the slice: x: 2, y: 2, z: 4, core: 2. Of those that a mesh axis runs over, the one named last changes fastest.
Arguments:
- inputs: bfloat16 [2, 128, 4096], P(None, ('tensor', 'dp')), may hold values from -6 to 6
- weights: bfloat16 [2, 4, 4096, 4096], P(None, 'pipe', None, 'tensor'), may hold values from -0.09375 to 0.09375
- norm_gains: float32 [2, 4, 4096], P(None, 'pipe'), may hold values from 0.1 to 1.9
- cotangent: bfloat16 [2, 128, 4096], P(None, ('tensor', 'dp')), may hold values from -6 to 6
Outputs:
- act_factor: bfloat16 [4096, 2, 4, 4096], P(('tensor', 'dp'), None, 'pipe')
- grad_factor: bfloat16 [4096, 2, 4, 4096], P(('tensor', 'dp'), None, 'pipe')
The draws below stay inside these ranges and needn't reach their ends.
All inputs are finite; a program needn't handle non-finite values.
Results may differ from the reference program's by a relative error of at most 0.025.
Values may be sent and summed in bfloat16 or wider, within the bound.
A program may use at most 192 MiB of HBM per device.

```python
import jax
import jax.numpy as jnp
from jax import lax

D = 4096
MB_DEV = 16
MICRO = 2
SLOTS = 2
LAYERS = 8
MICRO_TOKENS = 128
N_PIPE = 4
N_TENSOR = 4
N_DP = 2


def steps_of(own_key, dims, split, least, largest):
    def one(dim, parts):
        draws = jax.random.uniform(jax.random.fold_in(jax.random.fold_in(own_key, 6), dim), (parts,), jnp.float32, least / len(split), largest / len(split))
        return jnp.repeat(jnp.exp(draws), dims[dim] // parts).reshape((-1,) + (1,) * (len(dims) - dim - 1))

    loudness = one(*split[0])
    for cut in split[1:]:
        loudness = loudness * one(*cut)
    return loudness


def gaussian(key, shape, deviation, bound, split=(), dtype=jnp.bfloat16):
    array = deviation * jax.random.normal(key, shape, jnp.float32)
    if split:
        array = array * steps_of(key, shape, split, -0.22, 0.18)
    return jnp.clip(array, -bound, bound).astype(dtype)


def setup_inputs(seed: int = 0) -> dict:
    key_of = jax.random.split(jax.random.key(seed), 5)
    inputs = gaussian(key_of[0], (MICRO, MICRO_TOKENS, D), 1.0, 6.0, ((1, 8),))
    weights = gaussian(key_of[1], (SLOTS, N_PIPE, D, D), D ** -0.5, 0.09375, ((1, 4), (3, 4)))
    norm_gains = jnp.clip(1.0 + 0.18 * jax.random.normal(key_of[2], (SLOTS, N_PIPE, D), jnp.float32), 0.1, 1.9)
    cotangent = gaussian(key_of[3], (MICRO, MICRO_TOKENS, D), 1.0, 6.0, ((1, 8),))
    return {"inputs": inputs, "weights": weights, "norm_gains": norm_gains, "cotangent": cotangent}


EPSILON = 1e-05

def normalize(hidden, gain_row):
    hidden_wide = hidden.astype(jnp.float32)
    inverse_rms = lax.rsqrt(lax.optimization_barrier(jnp.mean(hidden_wide * hidden_wide, axis=-1, keepdims=True)) + EPSILON)
    normed = (hidden_wide * inverse_rms * gain_row).astype(jnp.bfloat16)
    return (hidden_wide, inverse_rms, normed)

def rounded(values):
    return lax.optimization_barrier(values.astype(jnp.bfloat16)).astype(jnp.float32)

def group_gram(tokens):
    grouped = tokens.reshape(MICRO, N_TENSOR, N_DP, MB_DEV, D)

    def add_group(group_pick, totals):
        chosen = lax.dynamic_index_in_dim(grouped, group_pick, 2, keepdims=False)
        flat_rows = chosen.reshape(MICRO * N_TENSOR * MB_DEV, D)
        gram = lax.dot_general(flat_rows, flat_rows, (((0,), (0,)), ((), ())), preferred_element_type=jnp.float32)
        return totals + rounded(gram * (1.0 / (MICRO * MICRO_TOKENS)))
    totals = lax.fori_loop(0, N_DP, add_group, jnp.zeros((D, D), jnp.float32))
    return totals.astype(jnp.bfloat16)

def reference(inputs, weights, norm_gains, cotangent):
    quarter = D // N_TENSOR
    hidden = inputs
    saved_hidden = []
    act_list = []
    for layer_index in range(LAYERS):
        slot_pick = layer_index // N_PIPE
        section_pick = layer_index % N_PIPE
        hidden_wide, inverse_rms, normed = normalize(hidden, norm_gains[slot_pick, section_pick])
        saved_hidden.append(hidden)
        act_list.append(group_gram(normed))
        if layer_index + 1 < LAYERS:
            product = jnp.dot(normed.reshape(-1, D), weights[slot_pick, section_pick], preferred_element_type=jnp.float32)
            product = product.astype(jnp.bfloat16).reshape(hidden.shape)
            hidden = (hidden_wide + product.astype(jnp.float32)).astype(jnp.bfloat16)
    delta = cotangent
    grad_list = [None] * LAYERS
    for layer_index in reversed(range(LAYERS)):
        grad_list[layer_index] = group_gram(delta)
        if layer_index > 0:
            slot_pick = layer_index // N_PIPE
            section_pick = layer_index % N_PIPE
            weight = weights[slot_pick, section_pick]
            gain_row = norm_gains[slot_pick, section_pick]
            flat_delta = delta.reshape(-1, D)
            back_sum = jnp.zeros(flat_delta.shape, jnp.float32)
            for column in range(N_TENSOR):
                lower = column * quarter
                upper = lower + quarter
                term = lax.dot_general(flat_delta[:, lower:upper], weight[:, lower:upper], (((1,), (1,)), ((), ())), preferred_element_type=jnp.float32)
                back_sum = back_sum + rounded(term)
            back_sum = back_sum.reshape(delta.shape)
            hidden_wide, inverse_rms, normed = normalize(saved_hidden[layer_index], gain_row)
            scaled = gain_row * back_sum
            inner = lax.optimization_barrier(jnp.mean(hidden_wide * scaled, axis=-1, keepdims=True))
            delta = (delta.astype(jnp.float32) + inverse_rms * scaled - inverse_rms ** 3 * hidden_wide * inner).astype(jnp.bfloat16)
    act_factor = jnp.stack(act_list, 0).reshape(SLOTS, N_PIPE, D, D).transpose(2, 0, 1, 3)
    grad_factor = jnp.stack(grad_list, 0).reshape(SLOTS, N_PIPE, D, D).transpose(2, 0, 1, 3)
    return (act_factor, grad_factor)
```

```python
import functools

import jax
import jax.numpy as jnp
from jax import lax
from jax.experimental import pallas as pl
from jax.experimental.pallas import tpu as pltpu
from jax.sharding import PartitionSpec as P

EPSILON = 1e-05
SPLITS = 2
CUTS = 2


def peer_of(c, k):
    return lax.rem(c // 2 + k // 2, 2) * 2 + lax.rem(c + k, 2)


def chain_kernel(
    dims,
    x_ref,
    w_hbm,
    g_ref,
    cot_ref,
    h_out,
    d_out,
    w,
    hbuf,
    dcol,
    rms,
    acc,
    nxt,
    own,
    far_send,
    far_recv,
    near_send,
    near_recv,
    x_send,
    x_recv,
    dnext,
    isend,
    irecv,
    w_sem,
    own_sem,
    in_send,
    in_recv,
    f1_send,
    f1_recv,
    fx_send,
    fx_recv,
    b1_send,
    b1_recv,
    s3_send,
    s3_recv,
    s1_send,
    s1_recv,
    xc_send,
    xc_recv,
    is_send,
    is_recv,
    dp_send,
    dp_recv,
    dg_send,
    dg_recv,
    loc_sem,
):
    chunks, splits, slots, rows, width, quarter, pipes, tensors, dps, cuts = dims
    items = slots * chunks
    layers = slots * pipes
    group = tensors * rows
    cut = quarter // cuts
    p = lax.axis_index("pipe")
    c = lax.axis_index("tensor")
    d = lax.axis_index("dp")
    after = lax.rem(p + 1, pipes)
    before = lax.rem(p + pipes - 1, pipes)

    def where(pp, cc, dd):
        return {"pipe": pp, "tensor": cc, "dp": dd}

    def remote(src, dst, send, recv, target):
        return pltpu.make_async_remote_copy(
            src_ref=src,
            dst_ref=dst,
            send_sem=send,
            recv_sem=recv,
            device_id=target,
            device_id_type=pl.DeviceIdType.MESH,
        )

    def w_copy(s):
        return pltpu.make_async_copy(w_hbm.at[s, 0], w.at[s], w_sem.at[s])

    for s in range(slots):
        w_copy(s).start()

    barrier = pltpu.get_barrier_semaphore()
    partners = [where(p, peer_of(c, k), d) for k in range(1, tensors)]
    partners += [where(after, c, d), where(before, c, d)]
    partners += [
        where(p, peer_of(c, k), lax.rem(d + e, dps)) for e in range(1, dps) for k in range(tensors)
    ]
    for partner in partners:
        pl.semaphore_signal(
            barrier, inc=1, device_id=partner, device_id_type=pl.DeviceIdType.MESH
        )
    pl.semaphore_wait(barrier, len(partners))

    def row_ds(cc):
        return pl.ds(pl.multiple_of(cc * rows, rows), rows)

    def col_ds(cc):
        return pl.ds(pl.multiple_of(cc * quarter, quarter), quarter)

    def cut_ds(cc, r):
        return pl.ds(pl.multiple_of(cc * quarter + r * cut, cut), cut)

    def span(r):
        return slice(r * cut, (r + 1) * cut)

    def opening_src(src, buf, q, cc):
        m, t = q // splits, q % splits
        part = src.at[m, t * rows : (t + 1) * rows]
        return part if buf is hbuf else part.at[:, col_ds(cc)]

    def opening(src, buf, q, k):
        return remote(
            opening_src(src, buf, q, peer_of(c, k)),
            buf.at[q, row_ds(c)],
            in_send.at[q, k - 1],
            in_recv.at[q, k - 1],
            where(p, peer_of(c, k), d),
        )

    def opening_own(src, buf, q):
        return pltpu.make_async_copy(
            opening_src(src, buf, q, c), buf.at[q, row_ds(c)], own_sem.at[q]
        )

    def opening_all(src, buf):
        for q in range(chunks):
            for k in (2, 3, 1):
                opening(src, buf, q, k).start()
        for q in range(chunks):
            opening_own(src, buf, q).start()

    def opening_wait(src, buf, q):
        whole = src.at[0, 0:rows]
        for k in range(1, tensors):
            part = whole if buf is hbuf else whole.at[:, col_ds(c)]
            remote(
                part,
                buf.at[q, row_ds(c)],
                in_send.at[q, k - 1],
                in_recv.at[q, k - 1],
                where(p, peer_of(c, k), d),
            ).wait_recv()
        part = whole if buf is hbuf else whole.at[:, col_ds(c)]
        pltpu.make_async_copy(part, buf.at[q, row_ds(c)], own_sem.at[q]).wait()

    @pl.when(p == 0)
    def _():
        opening_all(x_ref, hbuf)

    @pl.when(p == pipes - 1)
    def _():
        opening_all(cot_ref, dcol)

    def to_dp(item, slot, q, k):
        return remote(
            hbuf.at[item],
            h_out.at[slot, d, q],
            dp_send.at[item, k - 1],
            dp_recv.at[item, k - 1],
            where(p, c, lax.rem(d + k, dps)),
        )

    def to_own(item, slot, q):
        return pltpu.make_async_copy(hbuf.at[item], h_out.at[slot, d, q], loc_sem.at[0, item])

    def h_shares(item, slot, q):
        to_own(item, slot, q).start()
        for k in range(1, dps):
            to_dp(item, slot, q, k).start()

    def d_own(item, slot, q):
        return pltpu.make_async_copy(
            dcol.at[item], d_out.at[slot, d, q, :, col_ds(c)], loc_sem.at[1, item]
        )

    def d_share(item, slot, q, e, k):
        return remote(
            dcol.at[item],
            d_out.at[slot, d, q, :, col_ds(c)],
            dg_send.at[item, e, k],
            dg_recv.at[item, e, k],
            where(p, peer_of(c, k), lax.rem(d + e, dps)),
        )

    def d_shares(item, slot, q):
        return [
            d_share(item, slot, q, e, k)
            for e in range(dps - 1, -1, -1)
            for k in range(tensors - 1, -1, -1)
            if e or k
        ]

    def f_along(item, target_item, r):
        return remote(
            nxt.at[item, :, span(r)],
            hbuf.at[target_item, :, cut_ds(c, r)],
            f1_send.at[item, r],
            f1_recv.at[target_item, r],
            where(after, c, d),
        )

    def spread(item, part, r):
        owner = peer_of(c, 2) if part == 2 else c
        target = peer_of(c, 2) if part == 1 else peer_of(c, 1)
        ref = hbuf.at[item, :, cut_ds(owner, r)]
        return remote(
            ref, ref, fx_send.at[item, part, r], fx_recv.at[item, part, r], where(p, target, d)
        )

    def b_along(item, target_item, r):
        return remote(
            dnext.at[item, :, span(r)],
            dcol.at[target_item, :, span(r)],
            b1_send.at[item, r],
            b1_recv.at[target_item, r],
            where(before, c, d),
        )

    def far_copy(item, r):
        return remote(
            far_send.at[item, :, span(r)],
            far_recv.at[item, :, span(r)],
            s3_send.at[item, r],
            s3_recv.at[item, r],
            where(p, peer_of(c, 1), d),
        )

    def near_copy(item, r):
        return remote(
            near_send.at[item, :, span(r)],
            near_recv.at[item, :, span(r)],
            s1_send.at[item, r],
            s1_recv.at[item, r],
            where(p, peer_of(c, 1), d),
        )

    def x_copy(item, r):
        return remote(
            x_send.at[item, :, span(r)],
            x_recv.at[item, :, span(r)],
            xc_send.at[item, r],
            xc_recv.at[item, r],
            where(p, peer_of(c, 2), d),
        )

    def inner_copy(item, k):
        return remote(
            isend.at[item],
            irecv.at[item, k - 1],
            is_send.at[item, k - 1],
            is_recv.at[item, k - 1],
            where(p, peer_of(c, k), d),
        )

    def sums_start(item, first, second):
        lanes = [jnp.broadcast_to(v, (group, 128)) for v in (first, second)]
        square = jnp.concatenate([lanes[i % 2] for i in range(128 // group)], axis=0)
        isend[item] = jnp.transpose(square)[:8]
        for k in range(tensors - 1, 0, -1):
            inner_copy(item, k).start()

    def sums_finish(item):
        for k in range(1, tensors):
            inner_copy(item, k).wait_recv()
        sums = isend[item]
        for k in range(1, tensors):
            sums += irecv[item, k - 1]
        upright = jnp.transpose(jnp.concatenate([sums] * 16, axis=0))
        return upright[:group, :1], upright[group : 2 * group, :1]

    def reduce(item, slot, stored):
        columns = dcol[item]
        inner = jnp.zeros((group, 1), jnp.float32)
        order = [(3, r) for r in range(cuts)] + [(1, 0)] + [(2, r) for r in range(cuts)]
        order += [(1, r) for r in range(1, cuts)] + [(0, r) for r in range(cuts)]
        for k, r in order:
            where_to = cut_ds(peer_of(c, k), r)
            term = lax.dot_general(
                columns,
                w[slot, where_to, :],
                (((1,), (1,)), ((), ())),
                preferred_element_type=jnp.float32,
            ).astype(jnp.bfloat16)
            if k == 3:
                far_send[item, :, span(r)] = term
                far_copy(item, r).start()
            elif k == 2:
                far_copy(item, r).wait_recv()
                x_send[item, :, span(r)] = (
                    term.astype(jnp.float32) + far_recv[item, :, span(r)].astype(jnp.float32)
                ).astype(jnp.bfloat16)
                x_copy(item, r).start()
            elif k == 1:
                near_send[item, :, span(r)] = term
                near_copy(item, r).start()
            else:
                own[item, :, span(r)] = term
            if stored is not None:
                scaled = g_ref[slot, :, where_to] * term.astype(jnp.float32)
                hidden = hbuf[stored, :, where_to].astype(jnp.float32)
                inner += jnp.sum(hidden * scaled, axis=-1, keepdims=True)
        return inner

    def reduce_wait(item, r):
        near_copy(item, r).wait_recv()
        x_copy(item, r).wait_recv()

    def back_of(item, r):
        return (
            own[item, :, span(r)].astype(jnp.float32)
            + near_recv[item, :, span(r)].astype(jnp.float32)
            + x_recv[item, :, span(r)].astype(jnp.float32)
        )

    def finalize(item, slot, stored, inner_all, inverse_rms, waiting):
        factor = inverse_rms * inverse_rms * inverse_rms * (inner_all * (1.0 / width))
        target_item = item + chunks * (1 - (p + pipes - 1) // pipes)
        for r in range(cuts):
            if waiting:
                reduce_wait(item, r)
            dnext[item, :, span(r)] = (
                dcol[item, :, span(r)].astype(jnp.float32)
                + inverse_rms * (g_ref[slot, :, cut_ds(c, r)] * back_of(item, r))
                - factor * hbuf[stored, :, cut_ds(c, r)].astype(jnp.float32)
            ).astype(jnp.bfloat16)
            b_along(item, target_item, r).start()

    def turn_ahead(q, carry):
        opening_wait(cot_ref, dcol, q)
        d_own(q, slots - 1, q).start()
        reduce(q, slots - 1, None)
        for r in range(cuts):
            reduce_wait(q, r)
        return carry

    def turn_after(q, carry):
        item = (slots - 1) * chunks + q
        for r in range(cuts):
            spread(item, 1, r).wait_recv()
            spread(item, 2, r).start()
        for r in range(cuts):
            spread(item, 0, r).wait_recv()
            spread(item, 2, r).wait_recv()
        h_shares(item, slots - 1, q)
        for share in d_shares(q, slots - 1, q):
            share.start()
        return carry

    def f_step(item, carry):
        slot = item // chunks
        q = lax.rem(item, chunks)
        layer = slot * pipes + p
        target_item = item + chunks * ((p + 1) // pipes)

        @pl.when((layer == layers - 1) & (q == 0))
        def _():
            w_copy(slots - 1).wait()
            lax.fori_loop(0, chunks, turn_ahead, 0)

        @pl.when((layer < layers - 1) & (q == 0))
        def _():
            w_copy(slot).wait()

        @pl.when(layer == 0)
        def _():
            opening_wait(x_ref, hbuf, item)

        @pl.when(layer > 0)
        def _():
            for r in range(cuts):
                f_along(item, item, r).wait_recv()
                spread(item, 1, r).start()
                spread(item, 0, r).start()

        @pl.when(layer < layers - 1)
        def _():
            def scaled_of(cc, r):
                part = hbuf[item, :, cut_ds(cc, r)].astype(jnp.float32)
                scaled = (part * g_ref[slot, :, cut_ds(cc, r)]).astype(jnp.bfloat16)
                return scaled, jnp.sum(part * part, axis=-1, keepdims=True)

            def piece(cc, r, first=False):
                scaled, square = scaled_of(cc, r)
                product = jnp.dot(
                    scaled, w[slot, cut_ds(cc, r), :], preferred_element_type=jnp.float32
                )
                if first:
                    acc[...] = product
                else:
                    acc[...] += product
                return square

            total = piece(c, 0, True)
            for r in range(1, cuts):
                total += piece(c, r)

            @pl.when(layer > 0)
            def _():
                for r in range(cuts):
                    spread(item, 0, r).wait_recv()

            for r in range(cuts):
                total += piece(peer_of(c, 1), r)

            for r in range(cuts):

                @pl.when(layer > 0)
                def _(r=r):
                    spread(item, 1, r).wait_recv()
                    spread(item, 2, r).start()

                total += piece(peer_of(c, 2), r)

            for r in range(cuts):

                @pl.when(layer > 0)
                def _(r=r):
                    spread(item, 2, r).wait_recv()

                if r < cuts - 1:
                    total += piece(peer_of(c, 3), r)

            last = cut_ds(peer_of(c, 3), cuts - 1)
            scaled, square = scaled_of(peer_of(c, 3), cuts - 1)
            inverse_rms = lax.rsqrt((total + square) * (1.0 / width) + EPSILON)
            for n in range(cuts):
                product = acc[:, span(n)] + jnp.dot(
                    scaled, w[slot, last, span(n)], preferred_element_type=jnp.float32
                )
                product = (product * inverse_rms).astype(jnp.bfloat16).astype(jnp.float32)
                nxt[item, :, span(n)] = (
                    hbuf[item, :, cut_ds(c, n)].astype(jnp.float32) + product
                ).astype(jnp.bfloat16)
                f_along(item, target_item, n).start()
            rms[item] = jnp.broadcast_to(inverse_rms, (group, 128))
            h_shares(item, slot, q)

        @pl.when(layer == layers - 1)
        def _():
            inner = jnp.zeros((group, 1), jnp.float32)
            square = jnp.zeros((group, 1), jnp.float32)
            for r in range(cuts):
                hidden = hbuf[item, :, cut_ds(c, r)].astype(jnp.float32)
                scaled = g_ref[slot, :, cut_ds(c, r)] * back_of(q, r)
                inner += jnp.sum(hidden * scaled, axis=-1, keepdims=True)
                square += jnp.sum(hidden * hidden, axis=-1, keepdims=True)
            sums_start(q, inner, square)
            inner_all, square_all = sums_finish(q)
            inverse_rms = lax.rsqrt(square_all * (1.0 / width) + EPSILON)
            finalize(q, slot, item, inner_all, inverse_rms, False)

        @pl.when((layer == layers - 1) & (q == chunks - 1))
        def _():
            lax.fori_loop(0, chunks, turn_after, 0)

        return carry

    lax.fori_loop(0, items, f_step, 0)

    def b_step(item, carry):
        slot = slots - 1 - item // chunks
        q = lax.rem(item, chunks)
        layer = slot * pipes + p
        stored = slot * chunks + q

        @pl.when(layer < layers - 1)
        def _():
            for r in range(cuts):
                b_along(item, item, r).wait_recv()

        @pl.when(layer == 0)
        def _():
            for share in d_shares(item, slot, q):
                share.start()

        @pl.when(layer < layers - 1)
        def _():
            d_own(item, slot, q).start()

        @pl.when((layer > 0) & (layer < layers - 1))
        def _():
            inner = reduce(item, slot, stored)
            sums_start(item, inner, inner)
            inner_all, _ = sums_finish(item)
            finalize(item, slot, stored, inner_all, rms[stored][:, :1], True)

        @pl.when((layer > 0) & (layer < layers - 1) & (q == chunks - 1))
        def _():
            for back in range(chunks):
                for share in d_shares(item - (chunks - 1) + back, slot, back):
                    share.start()

        return carry

    lax.fori_loop(0, items, b_step, 0)

    @pl.when(p == 0)
    def _():
        for q in range(chunks):
            for k in range(1, tensors):
                opening(x_ref, hbuf, q, k).wait_send()

    @pl.when(p == pipes - 1)
    def _():
        for q in range(chunks):
            for k in range(1, tensors):
                opening(cot_ref, dcol, q, k).wait_send()

    def ending(item, carry):
        f_slot = item // chunks
        b_slot = slots - 1 - item // chunks
        q = lax.rem(item, chunks)
        f_layer = f_slot * pipes + p
        b_layer = b_slot * pipes + p

        @pl.when(f_layer > 0)
        def _():
            for part in range(3):
                for r in range(cuts):
                    spread(item, part, r).wait_send()

        @pl.when(f_layer < layers - 1)
        def _():
            for r in range(cuts):
                f_along(item, item, r).wait_send()

        @pl.when(b_layer > 0)
        def _():
            for r in range(cuts):
                b_along(item, item, r).wait_send()
                far_copy(item, r).wait_send()
                near_copy(item, r).wait_send()
                x_copy(item, r).wait_send()
            for k in range(1, tensors):
                inner_copy(item, k).wait_send()

        to_own(item, f_slot, q).wait()
        d_own(item, b_slot, q).wait()
        for k in range(1, dps):
            to_dp(item, f_slot, q, k).wait()
        for share in d_shares(item, b_slot, q):
            share.wait()
        return carry

    lax.fori_loop(0, items, ending, 0)


def chain(inputs, weights, norm_gains, cotangent):
    micro, own_rows, width = inputs.shape
    slots = weights.shape[0]
    quarter = weights.shape[3]
    pipes = lax.axis_size("pipe")
    tensors = lax.axis_size("tensor")
    dps = lax.axis_size("dp")
    splits = SPLITS
    cuts = CUTS
    rows = own_rows // splits
    chunks = micro * splits
    items = slots * chunks
    group = tensors * rows
    dims = (chunks, splits, slots, rows, width, quarter, pipes, tensors, dps, cuts)
    vmem = pl.BlockSpec(memory_space=pltpu.VMEM)
    hbm = pl.BlockSpec(memory_space=pl.ANY)
    dma = pltpu.SemaphoreType.DMA
    out = jax.ShapeDtypeStruct((slots, dps, chunks, group, width), jnp.bfloat16)
    piece = pltpu.VMEM((items, group, quarter), jnp.bfloat16)
    return pl.pallas_call(
        functools.partial(chain_kernel, dims),
        out_shape=(out, out),
        in_specs=[vmem, hbm, vmem, vmem],
        out_specs=(hbm, hbm),
        scratch_shapes=[
            pltpu.VMEM((slots, width, quarter), jnp.bfloat16),
            pltpu.VMEM((items, group, width), jnp.bfloat16),
            piece,
            pltpu.VMEM((items, group, 128), jnp.float32),
            pltpu.VMEM((group, quarter), jnp.float32),
            piece,
            piece,
            piece,
            piece,
            piece,
            piece,
            piece,
            piece,
            piece,
            pltpu.VMEM((items, 8, 128), jnp.float32),
            pltpu.VMEM((items, tensors - 1, 8, 128), jnp.float32),
            dma((slots,)),
            dma((chunks,)),
            dma((chunks, tensors - 1)),
            dma((chunks, tensors - 1)),
            dma((items, cuts)),
            dma((items, cuts)),
            dma((items, 3, cuts)),
            dma((items, 3, cuts)),
            dma((items, cuts)),
            dma((items, cuts)),
            dma((items, cuts)),
            dma((items, cuts)),
            dma((items, cuts)),
            dma((items, cuts)),
            dma((items, cuts)),
            dma((items, cuts)),
            dma((items, tensors - 1)),
            dma((items, tensors - 1)),
            dma((items, dps - 1)),
            dma((items, dps - 1)),
            dma((items, dps, tensors)),
            dma((items, dps, tensors)),
            dma((2, items)),
        ],
        compiler_params=pltpu.CompilerParams(
            collective_id=0, has_side_effects=True, vmem_limit_bytes=56 * 1024 * 1024
        ),
        name="chain",
    )(inputs, weights, norm_gains, cotangent)


def gram_kernel(base_rows, scale, normalized, x_ref, g_ref, out_ref, full, mixed):
    slots, tokens, width = x_ref.shape
    block = out_ref.shape[0]
    step = pl.program_id(0)

    if normalized:

        @pl.when(step == 0)
        def _():
            for s in range(slots):
                for t in range(0, tokens, 32):
                    wide = x_ref[s, t : t + 32].astype(jnp.float32)
                    mean = jnp.mean(wide * wide, axis=-1, keepdims=True)
                    inverse_rms = lax.rsqrt(mean + EPSILON)
                    full[s, t : t + 32] = (wide * inverse_rms * g_ref[s]).astype(jnp.bfloat16)

    source = full if normalized else x_ref
    own = (lax.axis_index("tensor") * lax.axis_size("dp") + lax.axis_index("dp")) * base_rows
    start = pl.multiple_of(own + step * block, block)
    columns = [source[s, :, pl.ds(start, block)] for s in range(slots)]
    span = 512
    for n in range(width // span):
        cut = slice(n * span, (n + 1) * span)
        for s in range(slots):
            gram = lax.dot_general(
                columns[s],
                source[s, :, cut],
                (((0,), (0,)), ((), ())),
                preferred_element_type=jnp.float32,
            )
            for q in range(span // 128):
                mixed[q, pl.ds(s, block, slots), :] = gram[:, q * 128 : (q + 1) * 128] * scale
        for q in range(span // 128):
            lane = slice(n * span + q * 128, n * span + (q + 1) * 128)
            out_ref[:, :, lane] = mixed[q].astype(jnp.bfloat16).reshape(block, slots, 128)


def gram_call(block, gains, own_rows, normalized):
    slots, tokens, width = block.shape
    tile = min(128, own_rows)
    out = pl.pallas_call(
        functools.partial(gram_kernel, own_rows, 1.0 / tokens, normalized),
        grid=(own_rows // tile,),
        out_shape=jax.ShapeDtypeStruct((own_rows, slots, width), jnp.bfloat16),
        in_specs=[
            pl.BlockSpec(block.shape, lambda i: (0, 0, 0), pipeline_mode=pl.Buffered(1)),
            pl.BlockSpec(gains.shape, lambda i: (0, 0, 0), pipeline_mode=pl.Buffered(1)),
        ],
        out_specs=pl.BlockSpec((tile, slots, width), lambda i: (i, 0, 0)),
        scratch_shapes=[
            pltpu.VMEM((slots, tokens, width) if normalized else (slots, 8, 128), jnp.bfloat16),
            pltpu.VMEM((4, tile * slots, 128), jnp.float32),
        ],
        compiler_params=pltpu.CompilerParams(vmem_limit_bytes=min(62 << 20, (32 << 20) + 8 * block.size)),
        name="gram",
    )(block, gains)
    return out.reshape(own_rows, slots, 1, width)


def body(inputs, weights, norm_gains, cotangent):
    micro, rows, width = inputs.shape
    slots = weights.shape[0]
    quarter = weights.shape[3]
    tensors = lax.axis_size("tensor")
    dps = lax.axis_size("dp")
    own_rows = quarter // dps
    tokens = micro * rows * tensors * dps
    h_all, d_all = chain(inputs, weights, norm_gains, cotangent)
    h_all = h_all.reshape(slots, tokens, width)
    d_all = d_all.reshape(slots, tokens, width)
    act = gram_call(h_all, norm_gains, own_rows, True)
    return act, gram_call(d_all, norm_gains, own_rows, False)


def solution(mesh):
    in_specs = (
        P(None, ("tensor", "dp"), None),
        P(None, "pipe", None, "tensor"),
        P(None, "pipe", None),
        P(None, ("tensor", "dp"), None),
    )
    out_specs = (P(("tensor", "dp"), None, "pipe", None), P(("tensor", "dp"), None, "pipe", None))
    return jax.shard_map(body, mesh=mesh, in_specs=in_specs, out_specs=out_specs, check_vma=False)
```

```python
import functools

import jax
import jax.numpy as jnp
from jax import lax
from jax.experimental import pallas as pl
from jax.experimental.pallas import tpu as pltpu
from jax.sharding import PartitionSpec as P

EPSILON = 1e-05
SPLITS = 2
CUTS = 2


def peer_of(c, k):
    return lax.rem(c // 2 + k // 2, 2) * 2 + lax.rem(c + k, 2)


def chain_kernel(
    dims,
    x_ref,
    w_hbm,
    g_ref,
    cot_ref,
    h_out,
    d_out,
    w,
    hbuf,
    dcol,
    rms,
    acc,
    nxt,
    far_send,
    far_recv,
    near_send,
    near_recv,
    a_send,
    a_recv,
    b_send,
    b_recv,
    isend,
    irecv,
    tsend,
    trecv,
    w_sem,
    own_sem,
    in_send,
    in_recv,
    f1_send,
    f1_recv,
    fx_send,
    fx_recv,
    ab_send,
    ab_recv,
    s3_send,
    s3_recv,
    s1_send,
    s1_recv,
    is_send,
    is_recv,
    ts_send,
    ts_recv,
    dp_send,
    dp_recv,
    dg_send,
    dg_recv,
    dr_send,
    dr_recv,
    loc_sem,
):
    chunks, splits, slots, rows, width, quarter, pipes, tensors, dps, cuts = dims
    items = slots * chunks
    layers = slots * pipes
    group = tensors * rows
    cut = quarter // cuts
    p = lax.axis_index("pipe")
    c = lax.axis_index("tensor")
    d = lax.axis_index("dp")
    after = lax.rem(p + 1, pipes)
    before = lax.rem(p + pipes - 1, pipes)

    def where(pp, cc, dd):
        return {"pipe": pp, "tensor": cc, "dp": dd}

    def remote(src, dst, send, recv, target):
        return pltpu.make_async_remote_copy(
            src_ref=src,
            dst_ref=dst,
            send_sem=send,
            recv_sem=recv,
            device_id=target,
            device_id_type=pl.DeviceIdType.MESH,
        )

    def w_copy(s):
        return pltpu.make_async_copy(w_hbm.at[s, 0], w.at[s], w_sem.at[s])

    for s in range(slots):
        w_copy(s).start()

    barrier = pltpu.get_barrier_semaphore()
    partners = [where(p, peer_of(c, k), d) for k in range(1, tensors)]
    partners += [where(pp, peer_of(c, k), d) for pp in (after, before) for k in range(tensors)]
    partners += [
        where(p, peer_of(c, k), lax.rem(d + e, dps)) for e in range(1, dps) for k in range(tensors)
    ]
    for partner in partners:
        pl.semaphore_signal(
            barrier, inc=1, device_id=partner, device_id_type=pl.DeviceIdType.MESH
        )
    pl.semaphore_wait(barrier, len(partners))

    def row_ds(cc):
        return pl.ds(pl.multiple_of(cc * rows, rows), rows)

    def col_ds(cc):
        return pl.ds(pl.multiple_of(cc * quarter, quarter), quarter)

    def cut_ds(cc, r):
        return pl.ds(pl.multiple_of(cc * quarter + r * cut, cut), cut)

    def span(r):
        return slice(r * cut, (r + 1) * cut)

    def opening_src(src, buf, q, cc):
        m, t = q // splits, q % splits
        part = src.at[m, t * rows : (t + 1) * rows]
        return part if buf is hbuf else part.at[:, col_ds(cc)]

    def opening(src, buf, q, k):
        return remote(
            opening_src(src, buf, q, peer_of(c, k)),
            buf.at[q, row_ds(c)],
            in_send.at[q, k - 1],
            in_recv.at[q, k - 1],
            where(p, peer_of(c, k), d),
        )

    def opening_own(src, buf, q):
        return pltpu.make_async_copy(
            opening_src(src, buf, q, c), buf.at[q, row_ds(c)], own_sem.at[q]
        )

    def opening_all(src, buf):
        for q in range(chunks):
            for k in (2, 3, 1):
                opening(src, buf, q, k).start()
        for q in range(chunks):
            opening_own(src, buf, q).start()

    def opening_wait(src, buf, q):
        whole = src.at[0, 0:rows]
        for k in range(1, tensors):
            part = whole if buf is hbuf else whole.at[:, col_ds(c)]
            remote(
                part,
                buf.at[q, row_ds(c)],
                in_send.at[q, k - 1],
                in_recv.at[q, k - 1],
                where(p, peer_of(c, k), d),
            ).wait_recv()
        part = whole if buf is hbuf else whole.at[:, col_ds(c)]
        pltpu.make_async_copy(part, buf.at[q, row_ds(c)], own_sem.at[q]).wait()

    @pl.when(p == 0)
    def _():
        opening_all(x_ref, hbuf)

    @pl.when(p >= pipes - 2)
    def _():
        opening_all(cot_ref, dcol)

    def to_dp(item, slot, q, k):
        return remote(
            hbuf.at[item],
            h_out.at[slot, d, q],
            dp_send.at[item, k - 1],
            dp_recv.at[item, k - 1],
            where(p, c, lax.rem(d + k, dps)),
        )

    def to_own(item, slot, q):
        return pltpu.make_async_copy(hbuf.at[item], h_out.at[slot, d, q], loc_sem.at[0, item])

    def h_shares(item, slot, q):
        to_own(item, slot, q).start()
        for k in range(1, dps):
            to_dp(item, slot, q, k).start()

    def d_own(item, slot, q):
        return pltpu.make_async_copy(
            dcol.at[item], d_out.at[slot, d, q, :, col_ds(c)], loc_sem.at[1, item]
        )

    def d_share(item, slot, q, e, k):
        return remote(
            dcol.at[item],
            d_out.at[slot, d, q, :, col_ds(c)],
            dg_send.at[item, e, k],
            dg_recv.at[item, e, k],
            where(p, peer_of(c, k), lax.rem(d + e, dps)),
        )

    far_shares = [(e, k) for e in range(dps - 1, -1, -1) for k in (2, 0) if e or k]

    def d_shares(item, slot, q):
        return [d_share(item, slot, q, e, k) for e, k in far_shares + [(0, 1)]]

    def d_relay(item, slot, q, e, k, arriving=False):
        origin = peer_of(peer_of(c, 1), k) if arriving else peer_of(c, k)
        ref = d_out.at[slot, lax.rem(d + dps - e, dps), q, :, col_ds(origin)]
        return remote(
            ref, ref, dr_send.at[item, e, k], dr_recv.at[item, e, k], where(p, peer_of(c, 1), d)
        )

    def d_relays(item, slot, q):
        for e, k in far_shares:
            d_share(item, slot, q, e, k).wait_recv()
            d_relay(item, slot, q, e, k).start()

    def f_along(item, target_item, k, r):
        return remote(
            nxt.at[item, :, span(r)],
            hbuf.at[target_item, :, cut_ds(c, r)],
            f1_send.at[item, k // 2, r],
            f1_recv.at[target_item, k // 2, r],
            where(after, peer_of(c, k), d),
        )

    def f_arrive(item, k, r):
        ref = hbuf.at[item, :, cut_ds(peer_of(c, k), r)]
        remote(
            ref, ref, f1_send.at[item, k // 2, r], f1_recv.at[item, k // 2, r], where(after, c, d)
        ).wait_recv()
        spread(item, k, r).start()

    def spread(item, k, r, arriving=False):
        origin = peer_of(peer_of(c, 1), k) if arriving else peer_of(c, k)
        ref = hbuf.at[item, :, cut_ds(origin, r)]
        return remote(
            ref,
            ref,
            fx_send.at[item, k // 2, r],
            fx_recv.at[item, k // 2, r],
            where(p, peer_of(c, 1), d),
        )

    def ab_copy(item, target_item, k, r):
        src, dst = (b_send, b_recv) if k else (a_send, a_recv)
        return remote(
            src.at[item, :, span(r)],
            dst.at[target_item, :, span(r)],
            ab_send.at[item, k // 2, r],
            ab_recv.at[target_item, k // 2, r],
            where(before, peer_of(c, k), d),
        )

    def far_copy(item, r):
        return remote(
            far_send.at[item, :, span(r)],
            far_recv.at[item, :, span(r)],
            s3_send.at[item, r],
            s3_recv.at[item, r],
            where(p, peer_of(c, 1), d),
        )

    def near_copy(item, r):
        return remote(
            near_send.at[item, :, span(r)],
            near_recv.at[item, :, span(r)],
            s1_send.at[item, r],
            s1_recv.at[item, r],
            where(p, peer_of(c, 1), d),
        )

    def inner_copy(item, target_item, k):
        return remote(
            isend.at[item],
            irecv.at[target_item, k],
            is_send.at[item, k],
            is_recv.at[target_item, k],
            where(before, peer_of(c, k), d),
        )

    def turn_copy(q, k):
        return remote(
            tsend.at[q],
            trecv.at[q, k - 1],
            ts_send.at[q, k - 1],
            ts_recv.at[q, k - 1],
            where(p, peer_of(c, k), d),
        )

    def flat(first, second):
        lanes = [jnp.broadcast_to(v, (group, 128)) for v in (first, second)]
        square = jnp.concatenate([lanes[i % 2] for i in range(128 // group)], axis=0)
        return jnp.transpose(square)[:8]

    def upright(sums):
        tall = jnp.transpose(jnp.concatenate([sums] * 16, axis=0))
        return tall[:group, :1], tall[group : 2 * group, :1]

    def before_item(item):
        return item + chunks * (1 - (p + pipes - 1) // pipes)

    def reduce(item, slot, stored):
        ahead = stored is None
        columns = dcol[item]
        target_item = before_item(item)
        inner = jnp.zeros((group, 1), jnp.float32)
        if not ahead:
            inverse_rms = rms[stored][:, :1]
        order = [(3, r) for r in range(cuts)] + [(1, 0)] + [(2, r) for r in range(cuts)]
        order += [(1, r) for r in range(1, cuts)] + [(0, r) for r in range(cuts)]
        for k, r in order:
            where_to = cut_ds(peer_of(c, k), r)
            gain = g_ref[slot, :, where_to]
            term = lax.dot_general(
                columns,
                w[slot, where_to, :],
                (((1,), (1,)), ((), ())),
                preferred_element_type=jnp.float32,
            )
            if k == 3:
                far_send[item, :, span(r)] = term.astype(jnp.bfloat16)
                far_copy(item, r).start()
            elif k == 1:
                near_send[item, :, span(r)] = term.astype(jnp.bfloat16)
                near_copy(item, r).start()
            elif k == 2:
                far_copy(item, r).wait_recv()
                both = gain * (term + far_recv[item, :, span(r)].astype(jnp.float32))
                if not ahead:
                    both = inverse_rms * both
                b_send[item, :, span(r)] = both.astype(jnp.bfloat16)
                ab_copy(item, target_item, 2, r).start()
            else:
                near_copy(item, r).wait_recv()
                both = gain * (term + near_recv[item, :, span(r)].astype(jnp.float32))
                if not ahead:
                    both = dcol[item, :, span(r)].astype(jnp.float32) + inverse_rms * both
                a_send[item, :, span(r)] = both.astype(jnp.bfloat16)
                ab_copy(item, target_item, 0, r).start()
            if not ahead:
                hidden = hbuf[stored, :, where_to].astype(jnp.float32)
                inner += jnp.sum(hidden * (gain * term), axis=-1, keepdims=True)
        if not ahead:
            factor = inverse_rms * inverse_rms * inverse_rms * (inner * (1.0 / width))
            isend[item] = flat(factor, factor)
            for k in (2, 3, 0, 1):
                inner_copy(item, target_item, k).start()

    def turn_ahead(q, carry):
        opening_wait(cot_ref, dcol, q)
        reduce(q, slots - 1, None)
        return carry

    def step(t, carry):
        f_on = t < items
        item = jnp.minimum(t, items - 1)
        slot = item // chunks
        q = lax.rem(item, chunks)
        layer = slot * pipes + p
        target_item = item + chunks * ((p + 1) // pipes)

        @pl.when(f_on & (layer == layers - 1) & (q == 0))
        def _():
            w_copy(slots - 1).wait()
            lax.fori_loop(0, chunks, turn_ahead, 0)

        @pl.when(f_on & (layer < layers - 1) & (q == 0))
        def _():
            w_copy(slot).wait()

        @pl.when(f_on & (layer == 0))
        def _():
            opening_wait(x_ref, hbuf, item)

        @pl.when(f_on & (layer > 0))
        def _():
            for r in range(cuts):
                f_arrive(item, 0, r)

        @pl.when(f_on & (layer < layers - 1))
        def _():
            def scaled_of(cc, r):
                part = hbuf[item, :, cut_ds(cc, r)].astype(jnp.float32)
                scaled = (part * g_ref[slot, :, cut_ds(cc, r)]).astype(jnp.bfloat16)
                return scaled, jnp.sum(part * part, axis=-1, keepdims=True)

            def piece(cc, r, first=False):
                scaled, square = scaled_of(cc, r)
                product = jnp.dot(
                    scaled, w[slot, cut_ds(cc, r), :], preferred_element_type=jnp.float32
                )
                if first:
                    acc[...] = product
                else:
                    acc[...] += product
                return square

            total = piece(c, 0, True)
            for r in range(1, cuts):
                total += piece(c, r)
            for r in range(cuts):

                @pl.when(layer > 0)
                def _(r=r):
                    f_arrive(item, 2, r)

                total += piece(peer_of(c, 2), r)
            for r in range(cuts):

                @pl.when(layer > 0)
                def _(r=r):
                    spread(item, 0, r, True).wait_recv()

                total += piece(peer_of(c, 1), r)
            for r in range(cuts):

                @pl.when(layer > 0)
                def _(r=r):
                    spread(item, 2, r, True).wait_recv()

                if r < cuts - 1:
                    total += piece(peer_of(c, 3), r)

            last = cut_ds(peer_of(c, 3), cuts - 1)
            scaled, square = scaled_of(peer_of(c, 3), cuts - 1)
            inverse_rms = lax.rsqrt((total + square) * (1.0 / width) + EPSILON)
            for n in range(cuts):
                product = acc[:, span(n)] + jnp.dot(
                    scaled, w[slot, last, span(n)], preferred_element_type=jnp.float32
                )
                product = (product * inverse_rms).astype(jnp.bfloat16).astype(jnp.float32)
                nxt[item, :, span(n)] = (
                    hbuf[item, :, cut_ds(c, n)].astype(jnp.float32) + product
                ).astype(jnp.bfloat16)
                f_along(item, target_item, 2, n).start()
                f_along(item, target_item, 0, n).start()
            rms[item] = jnp.broadcast_to(inverse_rms, (group, 128))

        @pl.when(f_on & (layer == layers - 2))
        def _():
            opening_wait(cot_ref, dcol, q)
            inner = jnp.zeros((group, 1), jnp.float32)
            square = jnp.zeros((group, 1), jnp.float32)
            for r in range(cuts):
                for k in (0, 2):
                    ab_copy(q, q, k, r).wait_recv()
                hidden = nxt[item, :, span(r)].astype(jnp.float32)
                back = a_recv[q, :, span(r)].astype(jnp.float32)
                back += b_recv[q, :, span(r)].astype(jnp.float32)
                inner += jnp.sum(hidden * back, axis=-1, keepdims=True)
                square += jnp.sum(hidden * hidden, axis=-1, keepdims=True)
            tsend[q] = flat(inner, square)
            for k in (2, 3, 1):
                turn_copy(q, k).start()

        @pl.when(f_on & (layer == layers - 1))
        def _():
            for r in range(cuts):
                f_arrive(item, 2, r)
            for r in range(cuts):
                spread(item, 0, r, True).wait_recv()
                spread(item, 2, r, True).wait_recv()

        @pl.when(f_on)
        def _():
            h_shares(item, slot, q)

        b_step(t)
        return carry

    def b_step(t):
        early = jnp.where(p == pipes - 2, chunks - 1, 0)
        b_time = t - (items - early)
        b_on = (b_time >= 0) & (b_time < items)
        item = jnp.clip(b_time, 0, items - 1)
        slot = slots - 1 - item // chunks
        q = lax.rem(item, chunks)
        layer = slot * pipes + p
        stored = slot * chunks + q

        @pl.when(b_on & (q == 0) & (slot < slots - 1))
        def _():
            for back in range(chunks):
                d_relays(item - chunks + back, slot + 1, back)

        @pl.when(b_on & (layer == layers - 2))
        def _():
            for k in range(1, tensors):
                turn_copy(q, k).wait_recv()
            sums = tsend[q]
            for k in range(1, tensors):
                sums += trecv[q, k - 1]
            inner, square = upright(sums)
            inverse_rms = lax.rsqrt(square * (1.0 / width) + EPSILON)
            factor = inverse_rms * inverse_rms * inverse_rms * (inner * (1.0 / width))
            for r in range(cuts):
                back = a_recv[item, :, span(r)].astype(jnp.float32)
                back += b_recv[item, :, span(r)].astype(jnp.float32)
                dcol[item, :, span(r)] = (
                    dcol[item, :, span(r)].astype(jnp.float32)
                    + inverse_rms * back
                    - factor * nxt[stored, :, span(r)].astype(jnp.float32)
                ).astype(jnp.bfloat16)

        @pl.when(b_on & (layer < layers - 2))
        def _():
            for k in range(tensors):
                inner_copy(item, item, k).wait_recv()
            sums = irecv[item, 0]
            for k in range(1, tensors):
                sums += irecv[item, k]
            factor, _ = upright(sums)
            for r in range(cuts):
                for k in (2, 0):
                    ab_copy(item, item, k, r).wait_recv()
                dcol[item, :, span(r)] = (
                    a_recv[item, :, span(r)].astype(jnp.float32)
                    + b_recv[item, :, span(r)].astype(jnp.float32)
                    - factor * nxt[stored, :, span(r)].astype(jnp.float32)
                ).astype(jnp.bfloat16)

        @pl.when(b_on & (layer > 0) & (layer < layers - 1))
        def _():
            reduce(item, slot, stored)

        @pl.when(b_on & (layer == 0))
        def _():
            for share in d_shares(item, slot, q):
                share.start()
            d_own(item, slot, q).start()

        @pl.when(b_on & (layer > 0) & (q == chunks - 1))
        def _():
            for back in range(chunks):
                for share in d_shares(item - (chunks - 1) + back, slot, back):
                    share.start()
                d_own(item - (chunks - 1) + back, slot, back).start()

    lax.fori_loop(0, 2 * items, step, 0)

    for back in range(chunks):
        d_relays((slots - 1) * chunks + back, 0, back)

    @pl.when(p == 0)
    def _():
        for q in range(chunks):
            for k in range(1, tensors):
                opening(x_ref, hbuf, q, k).wait_send()

    @pl.when(p >= pipes - 2)
    def _():
        for q in range(chunks):
            for k in range(1, tensors):
                opening(cot_ref, dcol, q, k).wait_send()

    def ending(item, carry):
        f_slot = item // chunks
        b_slot = slots - 1 - item // chunks
        q = lax.rem(item, chunks)
        f_layer = f_slot * pipes + p
        b_layer = b_slot * pipes + p

        @pl.when(f_layer > 0)
        def _():
            for k in (0, 2):
                for r in range(cuts):
                    spread(item, k, r).wait_send()

        @pl.when(f_layer < layers - 1)
        def _():
            for k in (0, 2):
                for r in range(cuts):
                    f_along(item, item, k, r).wait_send()

        @pl.when(b_layer > 0)
        def _():
            for r in range(cuts):
                for k in (0, 2):
                    ab_copy(item, item, k, r).wait_send()
                far_copy(item, r).wait_send()
                near_copy(item, r).wait_send()

        @pl.when((b_layer > 0) & (b_layer < layers - 1))
        def _():
            for k in range(tensors):
                inner_copy(item, item, k).wait_send()

        @pl.when(b_layer == layers - 2)
        def _():
            for k in range(1, tensors):
                turn_copy(q, k).wait_send()

        to_own(item, f_slot, q).wait()
        d_own(item, b_slot, q).wait()
        for k in range(1, dps):
            to_dp(item, f_slot, q, k).wait()
        for e, k in far_shares:
            d_share(item, b_slot, q, e, k).wait_send()
            d_relay(item, b_slot, q, e, k).wait_send()
            d_relay(item, b_slot, q, e, k, True).wait_recv()
        d_share(item, b_slot, q, 0, 1).wait()
        return carry

    lax.fori_loop(0, items, ending, 0)


def chain(inputs, weights, norm_gains, cotangent):
    micro, own_rows, width = inputs.shape
    slots = weights.shape[0]
    quarter = weights.shape[3]
    pipes = lax.axis_size("pipe")
    tensors = lax.axis_size("tensor")
    dps = lax.axis_size("dp")
    splits = SPLITS
    cuts = CUTS
    rows = own_rows // splits
    chunks = micro * splits
    items = slots * chunks
    group = tensors * rows
    dims = (chunks, splits, slots, rows, width, quarter, pipes, tensors, dps, cuts)
    vmem = pl.BlockSpec(memory_space=pltpu.VMEM)
    hbm = pl.BlockSpec(memory_space=pl.ANY)
    dma = pltpu.SemaphoreType.DMA
    out = jax.ShapeDtypeStruct((slots, dps, chunks, group, width), jnp.bfloat16)
    piece = pltpu.VMEM((items, group, quarter), jnp.bfloat16)
    return pl.pallas_call(
        functools.partial(chain_kernel, dims),
        out_shape=(out, out),
        in_specs=[vmem, hbm, vmem, vmem],
        out_specs=(hbm, hbm),
        scratch_shapes=[
            pltpu.VMEM((slots, width, quarter), jnp.bfloat16),
            pltpu.VMEM((items, group, width), jnp.bfloat16),
            piece,
            pltpu.VMEM((items, group, 128), jnp.float32),
            pltpu.VMEM((group, quarter), jnp.float32),
            piece,
            piece,
            piece,
            piece,
            piece,
            piece,
            piece,
            piece,
            piece,
            pltpu.VMEM((items, 8, 128), jnp.float32),
            pltpu.VMEM((items, tensors, 8, 128), jnp.float32),
            pltpu.VMEM((chunks, 8, 128), jnp.float32),
            pltpu.VMEM((chunks, tensors - 1, 8, 128), jnp.float32),
            dma((slots,)),
            dma((chunks,)),
            dma((chunks, tensors - 1)),
            dma((chunks, tensors - 1)),
            dma((items, 2, cuts)),
            dma((items, 2, cuts)),
            dma((items, 2, cuts)),
            dma((items, 2, cuts)),
            dma((items, 2, cuts)),
            dma((items, 2, cuts)),
            dma((items, cuts)),
            dma((items, cuts)),
            dma((items, cuts)),
            dma((items, cuts)),
            dma((items, tensors)),
            dma((items, tensors)),
            dma((chunks, tensors - 1)),
            dma((chunks, tensors - 1)),
            dma((items, dps - 1)),
            dma((items, dps - 1)),
            dma((items, dps, tensors)),
            dma((items, dps, tensors)),
            dma((items, dps, tensors)),
            dma((items, dps, tensors)),
            dma((2, items)),
        ],
        compiler_params=pltpu.CompilerParams(
            collective_id=0, has_side_effects=True, vmem_limit_bytes=56 * 1024 * 1024
        ),
        name="chain",
    )(inputs, weights, norm_gains, cotangent)


def gram_kernel(base_rows, scale, normalized, x_ref, g_ref, out_ref, full, mixed):
    slots, tokens, width = x_ref.shape
    block = out_ref.shape[0]
    step = pl.program_id(0)

    if normalized:

        @pl.when(step == 0)
        def _():
            for s in range(slots):
                for t in range(0, tokens, 32):
                    wide = x_ref[s, t : t + 32].astype(jnp.float32)
                    mean = jnp.mean(wide * wide, axis=-1, keepdims=True)
                    inverse_rms = lax.rsqrt(mean + EPSILON)
                    full[s, t : t + 32] = (wide * inverse_rms * g_ref[s]).astype(jnp.bfloat16)

    source = full if normalized else x_ref
    own = (lax.axis_index("tensor") * lax.axis_size("dp") + lax.axis_index("dp")) * base_rows
    start = pl.multiple_of(own + step * block, block)
    columns = [source[s, :, pl.ds(start, block)] for s in range(slots)]
    span = 512
    for n in range(width // span):
        cut = slice(n * span, (n + 1) * span)
        for s in range(slots):
            gram = lax.dot_general(
                columns[s],
                source[s, :, cut],
                (((0,), (0,)), ((), ())),
                preferred_element_type=jnp.float32,
            )
            for q in range(span // 128):
                mixed[q, pl.ds(s, block, slots), :] = gram[:, q * 128 : (q + 1) * 128] * scale
        for q in range(span // 128):
            lane = slice(n * span + q * 128, n * span + (q + 1) * 128)
            out_ref[:, :, lane] = mixed[q].astype(jnp.bfloat16).reshape(block, slots, 128)


def gram_call(block, gains, own_rows, normalized):
    slots, tokens, width = block.shape
    tile = min(128, own_rows)
    out = pl.pallas_call(
        functools.partial(gram_kernel, own_rows, 1.0 / tokens, normalized),
        grid=(own_rows // tile,),
        out_shape=jax.ShapeDtypeStruct((own_rows, slots, width), jnp.bfloat16),
        in_specs=[
            pl.BlockSpec(block.shape, lambda i: (0, 0, 0), pipeline_mode=pl.Buffered(1)),
            pl.BlockSpec(gains.shape, lambda i: (0, 0, 0), pipeline_mode=pl.Buffered(1)),
        ],
        out_specs=pl.BlockSpec((tile, slots, width), lambda i: (i, 0, 0)),
        scratch_shapes=[
            pltpu.VMEM((slots, tokens, width) if normalized else (slots, 8, 128), jnp.bfloat16),
            pltpu.VMEM((4, tile * slots, 128), jnp.float32),
        ],
        compiler_params=pltpu.CompilerParams(vmem_limit_bytes=min(62 << 20, (32 << 20) + 8 * block.size)),
        name="gram",
    )(block, gains)
    return out.reshape(own_rows, slots, 1, width)


def body(inputs, weights, norm_gains, cotangent):
    micro, rows, width = inputs.shape
    slots = weights.shape[0]
    quarter = weights.shape[3]
    tensors = lax.axis_size("tensor")
    dps = lax.axis_size("dp")
    own_rows = quarter // dps
    tokens = micro * rows * tensors * dps
    h_all, d_all = chain(inputs, weights, norm_gains, cotangent)
    h_all = h_all.reshape(slots, tokens, width)
    d_all = d_all.reshape(slots, tokens, width)
    act = gram_call(h_all, norm_gains, own_rows, True)
    return act, gram_call(d_all, norm_gains, own_rows, False)


def solution(mesh):
    in_specs = (
        P(None, ("tensor", "dp"), None),
        P(None, "pipe", None, "tensor"),
        P(None, "pipe", None),
        P(None, ("tensor", "dp"), None),
    )
    out_specs = (P(("tensor", "dp"), None, "pipe", None), P(("tensor", "dp"), None, "pipe", None))
    return jax.shard_map(body, mesh=mesh, in_specs=in_specs, out_specs=out_specs, check_vma=False)
```

```python
import functools

import jax
import jax.numpy as jnp
from jax import lax
from jax.experimental import pallas as pl
from jax.experimental.pallas import tpu as pltpu
from jax.sharding import PartitionSpec as P

EPSILON = 1e-05
SPLITS = 2
CUTS = 1


def peer_of(c, k):
    return lax.rem(c // 2 + k // 2, 2) * 2 + lax.rem(c + k, 2)


def chain_kernel(
    dims,
    x_ref,
    w_hbm,
    g_ref,
    cot_ref,
    h_out,
    d_out,
    w,
    w_t,
    hbuf,
    dcol,
    d_all,
    rms,
    acc,
    nxt,
    far_send,
    far_recv,
    near_send,
    near_recv,
    a_send,
    a_recv,
    b_send,
    b_recv,
    isend,
    irecv,
    tsend,
    trecv,
    w_sem,
    own_sem,
    in_send,
    in_recv,
    f1_send,
    f1_recv,
    fx_send,
    fx_recv,
    ab_send,
    ab_recv,
    s3_send,
    s3_recv,
    s1_send,
    s1_recv,
    is_send,
    is_recv,
    ts_send,
    ts_recv,
    dp_send,
    dp_recv,
    dg_send,
    dg_recv,
    dr_send,
    dr_recv,
    loc_sem,
):
    chunks, splits, slots, rows, width, quarter, pipes, tensors, dps, cuts = dims
    items = slots * chunks
    layers = slots * pipes
    group = tensors * rows
    cut = quarter // cuts
    p = lax.axis_index("pipe")
    c = lax.axis_index("tensor")
    d = lax.axis_index("dp")
    after = lax.rem(p + 1, pipes)
    before = lax.rem(p + pipes - 1, pipes)

    def where(pp, cc, dd):
        return {"pipe": pp, "tensor": cc, "dp": dd}

    def remote(src, dst, send, recv, target):
        return pltpu.make_async_remote_copy(
            src_ref=src,
            dst_ref=dst,
            send_sem=send,
            recv_sem=recv,
            device_id=target,
            device_id_type=pl.DeviceIdType.MESH,
        )

    def w_copy(s):
        return pltpu.make_async_copy(w_hbm.at[s, 0], w.at[s], w_sem.at[s])

    for s in range(slots):
        w_copy(s).start()

    barrier = pltpu.get_barrier_semaphore()
    partners = [where(p, peer_of(c, k), d) for k in range(1, tensors)]
    partners += [where(pp, peer_of(c, k), d) for pp in (after, before) for k in range(tensors)]
    partners += [
        where(p, peer_of(c, k), lax.rem(d + e, dps)) for e in range(1, dps) for k in range(tensors)
    ]
    for partner in partners:
        pl.semaphore_signal(
            barrier, inc=1, device_id=partner, device_id_type=pl.DeviceIdType.MESH
        )
    pl.semaphore_wait(barrier, len(partners))

    def row_ds(cc):
        return pl.ds(pl.multiple_of(cc * rows, rows), rows)

    def col_ds(cc):
        return pl.ds(pl.multiple_of(cc * quarter, quarter), quarter)

    def cut_ds(cc, r):
        return pl.ds(pl.multiple_of(cc * quarter + r * cut, cut), cut)

    def span(r):
        return slice(r * cut, (r + 1) * cut)

    def opening_src(src, buf, q, cc):
        m, t = q // splits, q % splits
        part = src.at[m, t * rows : (t + 1) * rows]
        return part if buf is hbuf else part.at[:, col_ds(cc)]

    def opening(src, buf, q, k):
        return remote(
            opening_src(src, buf, q, peer_of(c, k)),
            buf.at[q, row_ds(c)],
            in_send.at[q, k - 1],
            in_recv.at[q, k - 1],
            where(p, peer_of(c, k), d),
        )

    def opening_own(src, buf, q):
        return pltpu.make_async_copy(
            opening_src(src, buf, q, c), buf.at[q, row_ds(c)], own_sem.at[q]
        )

    def opening_all(src, buf):
        for q in range(chunks):
            for k in (2, 3, 1):
                opening(src, buf, q, k).start()
        for q in range(chunks):
            opening_own(src, buf, q).start()

    def opening_wait(src, buf, q):
        whole = src.at[0, 0:rows]
        for k in range(1, tensors):
            part = whole if buf is hbuf else whole.at[:, col_ds(c)]
            remote(
                part,
                buf.at[q, row_ds(c)],
                in_send.at[q, k - 1],
                in_recv.at[q, k - 1],
                where(p, peer_of(c, k), d),
            ).wait_recv()
        part = whole if buf is hbuf else whole.at[:, col_ds(c)]
        pltpu.make_async_copy(part, buf.at[q, row_ds(c)], own_sem.at[q]).wait()

    @pl.when(p == 0)
    def _():
        opening_all(x_ref, hbuf)

    @pl.when(p >= pipes - 2)
    def _():
        opening_all(cot_ref, dcol)

    def to_dp(item, slot, q, k):
        return remote(
            hbuf.at[item],
            h_out.at[slot, d, q],
            dp_send.at[item, k - 1],
            dp_recv.at[item, k - 1],
            where(p, c, lax.rem(d + k, dps)),
        )

    def to_own(item, slot, q):
        return pltpu.make_async_copy(hbuf.at[item], h_out.at[slot, d, q], loc_sem.at[0, item])

    def h_shares(item, slot, q):
        to_own(item, slot, q).start()
        for k in range(1, dps):
            to_dp(item, slot, q, k).start()

    def d_own(item, slot, q):
        return pltpu.make_async_copy(
            dcol.at[item], d_all.at[slot, d, q, :, col_ds(c)], loc_sem.at[1, item]
        )

    def d_share(item, slot, q, e, k):
        return remote(
            dcol.at[item],
            d_all.at[slot, d, q, :, col_ds(c)],
            dg_send.at[item, e, k],
            dg_recv.at[item, e, k],
            where(p, peer_of(c, k), lax.rem(d + e, dps)),
        )

    far_shares = [(e, k) for e in range(dps - 1, -1, -1) for k in (2, 0) if e or k]

    def d_shares(item, slot, q):
        return [d_share(item, slot, q, e, k) for e, k in far_shares + [(0, 1)]]

    def d_shares_all(first, slot):
        for q in range(chunks):
            for share in d_shares(first + q, slot, q):
                share.start()
            d_own(first + q, slot, q).start()

    def d_relay(item, slot, q, e, k, arriving=False):
        origin = peer_of(peer_of(c, 1), k) if arriving else peer_of(c, k)
        ref = d_all.at[slot, lax.rem(d + dps - e, dps), q, :, col_ds(origin)]
        return remote(
            ref, ref, dr_send.at[item, e, k], dr_recv.at[item, e, k], where(p, peer_of(c, 1), d)
        )

    def d_relays(item, slot, q):
        for e, k in far_shares:
            d_share(item, slot, q, e, k).wait_recv()
            d_relay(item, slot, q, e, k).start()

    def d_flush(item, slot, q):
        return pltpu.make_async_copy(
            d_all.at[slot, :, q], d_out.at[slot, :, q], loc_sem.at[2, item]
        )

    def d_gather(item, slot, q):
        d_own(item, slot, q).wait()
        for e, k in far_shares:
            d_relay(item, slot, q, e, k, True).wait_recv()
        d_share(item, slot, q, 0, 1).wait_recv()
        d_flush(item, slot, q).start()

    def f_along(item, target_item, k, r):
        return remote(
            nxt.at[item, :, span(r)],
            hbuf.at[target_item, :, cut_ds(c, r)],
            f1_send.at[item, k // 2, r],
            f1_recv.at[target_item, k // 2, r],
            where(after, peer_of(c, k), d),
        )

    def f_arrive(item, k, r):
        ref = hbuf.at[item, :, cut_ds(peer_of(c, k), r)]
        remote(
            ref, ref, f1_send.at[item, k // 2, r], f1_recv.at[item, k // 2, r], where(after, c, d)
        ).wait_recv()
        spread(item, k, r).start()

    def spread(item, k, r, arriving=False):
        origin = peer_of(peer_of(c, 1), k) if arriving else peer_of(c, k)
        ref = hbuf.at[item, :, cut_ds(origin, r)]
        return remote(
            ref,
            ref,
            fx_send.at[item, k // 2, r],
            fx_recv.at[item, k // 2, r],
            where(p, peer_of(c, 1), d),
        )

    def ab_copy(item, target_item, k, r):
        src, dst = (b_send, b_recv) if k else (a_send, a_recv)
        return remote(
            src.at[item, :, span(r)],
            dst.at[target_item, :, span(r)],
            ab_send.at[item, k // 2, r],
            ab_recv.at[target_item, k // 2, r],
            where(before, peer_of(c, k), d),
        )

    def far_copy(item, r):
        return remote(
            far_send.at[item, :, span(r)],
            far_recv.at[item, :, span(r)],
            s3_send.at[item, r],
            s3_recv.at[item, r],
            where(p, peer_of(c, 1), d),
        )

    def near_copy(item, r):
        return remote(
            near_send.at[item, :, span(r)],
            near_recv.at[item, :, span(r)],
            s1_send.at[item, r],
            s1_recv.at[item, r],
            where(p, peer_of(c, 1), d),
        )

    def inner_copy(item, target_item, k):
        return remote(
            isend.at[item],
            irecv.at[target_item, k],
            is_send.at[item, k],
            is_recv.at[target_item, k],
            where(before, peer_of(c, k), d),
        )

    def turn_copy(q, k):
        return remote(
            tsend.at[q],
            trecv.at[q, k - 1],
            ts_send.at[q, k - 1],
            ts_recv.at[q, k - 1],
            where(p, peer_of(c, k), d),
        )

    def flat(first, second):
        lanes = [jnp.broadcast_to(v, (group, 128)) for v in (first, second)]
        square = jnp.concatenate([lanes[i % 2] for i in range(128 // group)], axis=0)
        return jnp.transpose(square)[:8]

    def upright(sums):
        tall = jnp.transpose(jnp.concatenate([sums] * 16, axis=0))
        return tall[:group, :1], tall[group : 2 * group, :1]

    def before_item(item):
        return item + chunks * (1 - (p + pipes - 1) // pipes)

    def reduce(item, slot, stored):
        ahead = stored is None
        columns = dcol[item]
        target_item = before_item(item)
        inner = jnp.zeros((group, 1), jnp.float32)
        if not ahead:
            inverse_rms = rms[stored][:, :1]
        order = [(3, r) for r in range(cuts)] + [(1, 0)] + [(2, r) for r in range(cuts)]
        order += [(1, r) for r in range(1, cuts)] + [(0, r) for r in range(cuts)]
        for k, r in order:
            where_to = cut_ds(peer_of(c, k), r)
            gain = g_ref[slot, :, where_to]
            term = jnp.dot(columns, w_t[slot, :, where_to], preferred_element_type=jnp.float32)
            if k == 3:
                far_send[item, :, span(r)] = term.astype(jnp.bfloat16)
                far_copy(item, r).start()
            elif k == 1:
                near_send[item, :, span(r)] = term.astype(jnp.bfloat16)
                near_copy(item, r).start()
            elif k == 2:
                far_copy(item, r).wait_recv()
                both = gain * (term + far_recv[item, :, span(r)].astype(jnp.float32))
                if not ahead:
                    both = inverse_rms * both
                b_send[item, :, span(r)] = both.astype(jnp.bfloat16)
                ab_copy(item, target_item, 2, r).start()
            else:
                near_copy(item, r).wait_recv()
                both = gain * (term + near_recv[item, :, span(r)].astype(jnp.float32))
                if not ahead:
                    both = dcol[item, :, span(r)].astype(jnp.float32) + inverse_rms * both
                a_send[item, :, span(r)] = both.astype(jnp.bfloat16)
                ab_copy(item, target_item, 0, r).start()
            if not ahead:
                hidden = hbuf[stored, :, where_to].astype(jnp.float32)
                inner += jnp.sum(hidden * (gain * term), axis=-1, keepdims=True)
        if not ahead:
            factor = inverse_rms * inverse_rms * inverse_rms * (inner * (1.0 / width))
            isend[item] = flat(factor, factor)
            for k in (2, 3, 0, 1):
                inner_copy(item, target_item, k).start()

    def turn_over(s):
        side = 256

        def block(i, carry):
            part = pl.ds(pl.multiple_of(i * side, side), side)
            w_t[s, :, part] = jnp.transpose(w[s, part, :])
            return carry

        lax.fori_loop(0, width // side, block, 0)

    def turn_ahead(q, carry):
        opening_wait(cot_ref, dcol, q)
        reduce(q, slots - 1, None)
        return carry

    def step(t, carry):
        f_on = t < items
        item = jnp.minimum(t, items - 1)
        slot = item // chunks
        q = lax.rem(item, chunks)
        layer = slot * pipes + p
        target_item = item + chunks * ((p + 1) // pipes)

        @pl.when(f_on & (q == 0))
        def _():
            w_copy(slot).wait()

        @pl.when(f_on & (q == 0) & (slot == slots - 1))
        def _():
            turn_over(slots - 1)

            @pl.when(layer == layers - 1)
            def _():
                lax.fori_loop(0, chunks, turn_ahead, 0)
                d_shares_all(0, slots - 1)

            for s in range(slots - 1):
                turn_over(s)

        @pl.when(f_on & (layer == 0))
        def _():
            opening_wait(x_ref, hbuf, item)

        @pl.when(f_on & (layer > 0))
        def _():
            for r in range(cuts):
                f_arrive(item, 0, r)

        @pl.when(f_on & (layer < layers - 1))
        def _():
            def scaled_of(cc, r):
                part = hbuf[item, :, cut_ds(cc, r)].astype(jnp.float32)
                scaled = (part * g_ref[slot, :, cut_ds(cc, r)]).astype(jnp.bfloat16)
                return scaled, jnp.sum(part * part, axis=-1, keepdims=True)

            def piece(cc, r, first=False):
                scaled, square = scaled_of(cc, r)
                product = jnp.dot(
                    scaled, w[slot, cut_ds(cc, r), :], preferred_element_type=jnp.float32
                )
                if first:
                    acc[...] = product
                else:
                    acc[...] += product
                return square

            total = piece(c, 0, True)
            for r in range(1, cuts):
                total += piece(c, r)
            for r in range(cuts):

                @pl.when(layer > 0)
                def _(r=r):
                    f_arrive(item, 2, r)

                total += piece(peer_of(c, 2), r)
            for r in range(cuts):

                @pl.when(layer > 0)
                def _(r=r):
                    spread(item, 0, r, True).wait_recv()

                total += piece(peer_of(c, 1), r)
            for r in range(cuts):

                @pl.when(layer > 0)
                def _(r=r):
                    spread(item, 2, r, True).wait_recv()

                if r < cuts - 1:
                    total += piece(peer_of(c, 3), r)

            last = cut_ds(peer_of(c, 3), cuts - 1)
            scaled, square = scaled_of(peer_of(c, 3), cuts - 1)
            inverse_rms = lax.rsqrt((total + square) * (1.0 / width) + EPSILON)
            for n in range(cuts):
                product = acc[:, span(n)] + jnp.dot(
                    scaled, w[slot, last, span(n)], preferred_element_type=jnp.float32
                )
                product = (product * inverse_rms).astype(jnp.bfloat16).astype(jnp.float32)
                nxt[item, :, span(n)] = (
                    hbuf[item, :, cut_ds(c, n)].astype(jnp.float32) + product
                ).astype(jnp.bfloat16)
                f_along(item, target_item, 2, n).start()
                f_along(item, target_item, 0, n).start()
            rms[item] = jnp.broadcast_to(inverse_rms, (group, 128))

        @pl.when(f_on & (layer == layers - 2))
        def _():
            opening_wait(cot_ref, dcol, q)
            inner = jnp.zeros((group, 1), jnp.float32)
            square = jnp.zeros((group, 1), jnp.float32)
            for r in range(cuts):
                for k in (0, 2):
                    ab_copy(q, q, k, r).wait_recv()
                hidden = nxt[item, :, span(r)].astype(jnp.float32)
                back = a_recv[q, :, span(r)].astype(jnp.float32)
                back += b_recv[q, :, span(r)].astype(jnp.float32)
                inner += jnp.sum(hidden * back, axis=-1, keepdims=True)
                square += jnp.sum(hidden * hidden, axis=-1, keepdims=True)
            tsend[q] = flat(inner, square)
            for k in (2, 3, 1):
                turn_copy(q, k).start()

        @pl.when(f_on & (layer == layers - 1))
        def _():
            for r in range(cuts):
                f_arrive(item, 2, r)
            for r in range(cuts):
                spread(item, 0, r, True).wait_recv()
                spread(item, 2, r, True).wait_recv()

        @pl.when(f_on)
        def _():
            h_shares(item, slot, q)

        b_step(t)
        return carry

    def b_step(t):
        early = jnp.where(p == pipes - 2, chunks - 1, 0)
        b_time = t - (items - early)
        b_on = (b_time >= 0) & (b_time < items)
        item = jnp.clip(b_time, 0, items - 1)
        slot = slots - 1 - item // chunks
        q = lax.rem(item, chunks)
        layer = slot * pipes + p
        stored = slot * chunks + q

        @pl.when(b_on & (q == 0) & (slot < slots - 1))
        def _():
            for back in range(chunks):
                d_relays(item - chunks + back, slot + 1, back)
            for back in range(chunks):
                d_gather(item - chunks + back, slot + 1, back)

        @pl.when(b_on & (layer == layers - 2))
        def _():
            for k in range(1, tensors):
                turn_copy(q, k).wait_recv()
            sums = tsend[q]
            for k in range(1, tensors):
                sums += trecv[q, k - 1]
            inner, square = upright(sums)
            inverse_rms = lax.rsqrt(square * (1.0 / width) + EPSILON)
            factor = inverse_rms * inverse_rms * inverse_rms * (inner * (1.0 / width))
            for r in range(cuts):
                back = a_recv[item, :, span(r)].astype(jnp.float32)
                back += b_recv[item, :, span(r)].astype(jnp.float32)
                dcol[item, :, span(r)] = (
                    dcol[item, :, span(r)].astype(jnp.float32)
                    + inverse_rms * back
                    - factor * nxt[stored, :, span(r)].astype(jnp.float32)
                ).astype(jnp.bfloat16)

        @pl.when(b_on & (layer < layers - 2))
        def _():
            for k in range(tensors):
                inner_copy(item, item, k).wait_recv()
            sums = irecv[item, 0]
            for k in range(1, tensors):
                sums += irecv[item, k]
            factor, _ = upright(sums)
            for r in range(cuts):
                for k in (2, 0):
                    ab_copy(item, item, k, r).wait_recv()
                dcol[item, :, span(r)] = (
                    a_recv[item, :, span(r)].astype(jnp.float32)
                    + b_recv[item, :, span(r)].astype(jnp.float32)
                    - factor * nxt[stored, :, span(r)].astype(jnp.float32)
                ).astype(jnp.bfloat16)

        @pl.when(b_on & (layer > 0) & (layer < layers - 1))
        def _():
            reduce(item, slot, stored)

        @pl.when(b_on & (slot == 0))
        def _():
            for share in d_shares(item, slot, q):
                share.start()
            d_own(item, slot, q).start()

        @pl.when(b_on & (layer == 0) & (q > 0))
        def _():
            d_relays(item - 1, slot, q - 1)

        @pl.when(b_on & (slot > 0) & (layer < layers - 1) & (q == chunks - 1))
        def _():
            d_shares_all(item - (chunks - 1), slot)

    lax.fori_loop(0, 2 * items, step, 0)

    for q in range(chunks):
        item = (slots - 1) * chunks + q
        if q == chunks - 1:
            d_relays(item, 0, q)
        else:

            @pl.when(p > 0)
            def _(item=item, q=q):
                d_relays(item, 0, q)

    for q in range(chunks):
        d_gather((slots - 1) * chunks + q, 0, q)

    @pl.when(p == 0)
    def _():
        for q in range(chunks):
            for k in range(1, tensors):
                opening(x_ref, hbuf, q, k).wait_send()

    @pl.when(p >= pipes - 2)
    def _():
        for q in range(chunks):
            for k in range(1, tensors):
                opening(cot_ref, dcol, q, k).wait_send()

    def ending(item, carry):
        f_slot = item // chunks
        b_slot = slots - 1 - item // chunks
        q = lax.rem(item, chunks)
        f_layer = f_slot * pipes + p
        b_layer = b_slot * pipes + p

        @pl.when(f_layer > 0)
        def _():
            for k in (0, 2):
                for r in range(cuts):
                    spread(item, k, r).wait_send()

        @pl.when(f_layer < layers - 1)
        def _():
            for k in (0, 2):
                for r in range(cuts):
                    f_along(item, item, k, r).wait_send()

        @pl.when(b_layer > 0)
        def _():
            for r in range(cuts):
                for k in (0, 2):
                    ab_copy(item, item, k, r).wait_send()
                far_copy(item, r).wait_send()
                near_copy(item, r).wait_send()

        @pl.when((b_layer > 0) & (b_layer < layers - 1))
        def _():
            for k in range(tensors):
                inner_copy(item, item, k).wait_send()

        @pl.when(b_layer == layers - 2)
        def _():
            for k in range(1, tensors):
                turn_copy(q, k).wait_send()

        to_own(item, f_slot, q).wait()
        d_flush(item, b_slot, q).wait()
        for k in range(1, dps):
            to_dp(item, f_slot, q, k).wait()
        for e, k in far_shares:
            d_share(item, b_slot, q, e, k).wait_send()
            d_relay(item, b_slot, q, e, k).wait_send()
        d_share(item, b_slot, q, 0, 1).wait_send()
        return carry

    lax.fori_loop(0, items, ending, 0)


def chain(inputs, weights, norm_gains, cotangent):
    micro, own_rows, width = inputs.shape
    slots = weights.shape[0]
    quarter = weights.shape[3]
    pipes = lax.axis_size("pipe")
    tensors = lax.axis_size("tensor")
    dps = lax.axis_size("dp")
    splits = SPLITS
    cuts = CUTS
    rows = own_rows // splits
    chunks = micro * splits
    items = slots * chunks
    group = tensors * rows
    dims = (chunks, splits, slots, rows, width, quarter, pipes, tensors, dps, cuts)
    vmem = pl.BlockSpec(memory_space=pltpu.VMEM)
    hbm = pl.BlockSpec(memory_space=pl.ANY)
    dma = pltpu.SemaphoreType.DMA
    out = jax.ShapeDtypeStruct((slots, dps, chunks, group, width), jnp.bfloat16)
    piece = pltpu.VMEM((items, group, quarter), jnp.bfloat16)
    return pl.pallas_call(
        functools.partial(chain_kernel, dims),
        out_shape=(out, out),
        in_specs=[vmem, hbm, vmem, vmem],
        out_specs=(hbm, hbm),
        scratch_shapes=[
            pltpu.VMEM((slots, width, quarter), jnp.bfloat16),
            pltpu.VMEM((slots, quarter, width), jnp.bfloat16),
            pltpu.VMEM((items, group, width), jnp.bfloat16),
            piece,
            pltpu.VMEM((slots, dps, chunks, group, width), jnp.bfloat16),
            pltpu.VMEM((items, group, 128), jnp.float32),
            pltpu.VMEM((group, quarter), jnp.float32),
            piece,
            piece,
            piece,
            piece,
            piece,
            piece,
            piece,
            piece,
            piece,
            pltpu.VMEM((items, 8, 128), jnp.float32),
            pltpu.VMEM((items, tensors, 8, 128), jnp.float32),
            pltpu.VMEM((chunks, 8, 128), jnp.float32),
            pltpu.VMEM((chunks, tensors - 1, 8, 128), jnp.float32),
            dma((slots,)),
            dma((chunks,)),
            dma((chunks, tensors - 1)),
            dma((chunks, tensors - 1)),
            dma((items, 2, cuts)),
            dma((items, 2, cuts)),
            dma((items, 2, cuts)),
            dma((items, 2, cuts)),
            dma((items, 2, cuts)),
            dma((items, 2, cuts)),
            dma((items, cuts)),
            dma((items, cuts)),
            dma((items, cuts)),
            dma((items, cuts)),
            dma((items, tensors)),
            dma((items, tensors)),
            dma((chunks, tensors - 1)),
            dma((chunks, tensors - 1)),
            dma((items, dps - 1)),
            dma((items, dps - 1)),
            dma((items, dps, tensors)),
            dma((items, dps, tensors)),
            dma((items, dps, tensors)),
            dma((items, dps, tensors)),
            dma((3, items)),
        ],
        compiler_params=pltpu.CompilerParams(
            collective_id=0, has_side_effects=True, vmem_limit_bytes=62 * 1024 * 1024
        ),
        name="chain",
    )(inputs, weights, norm_gains, cotangent)


def gram_kernel(base_rows, scale, normalized, x_ref, g_ref, out_ref, full, mixed):
    slots, tokens, width = x_ref.shape
    block = out_ref.shape[0]
    step = pl.program_id(0)

    if normalized:

        @pl.when(step == 0)
        def _():
            for s in range(slots):
                for t in range(0, tokens, 32):
                    wide = x_ref[s, t : t + 32].astype(jnp.float32)
                    mean = jnp.mean(wide * wide, axis=-1, keepdims=True)
                    inverse_rms = lax.rsqrt(mean + EPSILON)
                    full[s, t : t + 32] = (wide * inverse_rms * g_ref[s]).astype(jnp.bfloat16)

    source = full if normalized else x_ref
    own = (lax.axis_index("tensor") * lax.axis_size("dp") + lax.axis_index("dp")) * base_rows
    start = pl.multiple_of(own + step * block, block)
    columns = [source[s, :, pl.ds(start, block)] for s in range(slots)]
    span = 512
    for n in range(width // span):
        cut = slice(n * span, (n + 1) * span)
        for s in range(slots):
            gram = lax.dot_general(
                columns[s],
                source[s, :, cut],
                (((0,), (0,)), ((), ())),
                preferred_element_type=jnp.float32,
            )
            for q in range(span // 128):
                mixed[q, pl.ds(s, block, slots), :] = gram[:, q * 128 : (q + 1) * 128] * scale
        for q in range(span // 128):
            lane = slice(n * span + q * 128, n * span + (q + 1) * 128)
            out_ref[:, :, lane] = mixed[q].astype(jnp.bfloat16).reshape(block, slots, 128)


def gram_call(block, gains, own_rows, normalized):
    slots, tokens, width = block.shape
    tile = min(128, own_rows)
    out = pl.pallas_call(
        functools.partial(gram_kernel, own_rows, 1.0 / tokens, normalized),
        grid=(own_rows // tile,),
        out_shape=jax.ShapeDtypeStruct((own_rows, slots, width), jnp.bfloat16),
        in_specs=[
            pl.BlockSpec(block.shape, lambda i: (0, 0, 0), pipeline_mode=pl.Buffered(1)),
            pl.BlockSpec(gains.shape, lambda i: (0, 0, 0), pipeline_mode=pl.Buffered(1)),
        ],
        out_specs=pl.BlockSpec((tile, slots, width), lambda i: (i, 0, 0)),
        scratch_shapes=[
            pltpu.VMEM((slots, tokens, width) if normalized else (slots, 8, 128), jnp.bfloat16),
            pltpu.VMEM((4, tile * slots, 128), jnp.float32),
        ],
        compiler_params=pltpu.CompilerParams(vmem_limit_bytes=min(62 << 20, (32 << 20) + 8 * block.size)),
        name="gram",
    )(block, gains)
    return out.reshape(own_rows, slots, 1, width)


def body(inputs, weights, norm_gains, cotangent):
    micro, rows, width = inputs.shape
    slots = weights.shape[0]
    quarter = weights.shape[3]
    tensors = lax.axis_size("tensor")
    dps = lax.axis_size("dp")
    own_rows = quarter // dps
    tokens = micro * rows * tensors * dps
    h_all, d_all = chain(inputs, weights, norm_gains, cotangent)
    h_all = h_all.reshape(slots, tokens, width)
    d_all = d_all.reshape(slots, tokens, width)
    act = gram_call(h_all, norm_gains, own_rows, True)
    return act, gram_call(d_all, norm_gains, own_rows, False)


def solution(mesh):
    in_specs = (
        P(None, ("tensor", "dp"), None),
        P(None, "pipe", None, "tensor"),
        P(None, "pipe", None),
        P(None, ("tensor", "dp"), None),
    )
    out_specs = (P(("tensor", "dp"), None, "pipe", None), P(("tensor", "dp"), None, "pipe", None))
    return jax.shard_map(body, mesh=mesh, in_specs=in_specs, out_specs=out_specs, check_vma=False)
```

```python
import functools

import jax
import jax.numpy as jnp
from jax import lax
from jax.experimental import pallas as pl
from jax.experimental.pallas import tpu as pltpu
from jax.sharding import PartitionSpec as P

EPSILON = 1e-05
SPLITS = 2
CUTS = 1
SPAN = 1024


def peer_of(c, k):
    return lax.rem(c // 2 + k // 2, 2) * 2 + lax.rem(c + k, 2)


def chain_kernel(
    dims,
    x_ref,
    w_hbm,
    g_ref,
    cot_ref,
    h_out,
    d_out,
    w,
    w_t,
    hbuf,
    normed,
    dcol,
    d_all,
    rms,
    acc,
    nxt,
    far_send,
    far_recv,
    near_send,
    near_recv,
    a_send,
    a_recv,
    b_send,
    b_recv,
    isend,
    irecv,
    tsend,
    trecv,
    w_sem,
    own_sem,
    in_send,
    in_recv,
    f1_send,
    f1_recv,
    fx_send,
    fx_recv,
    ab_send,
    ab_recv,
    s3_send,
    s3_recv,
    s1_send,
    s1_recv,
    is_send,
    is_recv,
    ts_send,
    ts_recv,
    dp_send,
    dp_recv,
    dg_send,
    dg_recv,
    dr_send,
    dr_recv,
    loc_sem,
):
    chunks, splits, slots, rows, width, quarter, pipes, tensors, dps, cuts = dims
    items = slots * chunks
    layers = slots * pipes
    group = tensors * rows
    cut = quarter // cuts
    p = lax.axis_index("pipe")
    c = lax.axis_index("tensor")
    d = lax.axis_index("dp")
    after = lax.rem(p + 1, pipes)
    before = lax.rem(p + pipes - 1, pipes)

    def where(pp, cc, dd):
        return {"pipe": pp, "tensor": cc, "dp": dd}

    def remote(src, dst, send, recv, target):
        return pltpu.make_async_remote_copy(
            src_ref=src,
            dst_ref=dst,
            send_sem=send,
            recv_sem=recv,
            device_id=target,
            device_id_type=pl.DeviceIdType.MESH,
        )

    def w_copy(s):
        return pltpu.make_async_copy(w_hbm.at[s, 0], w.at[s], w_sem.at[s])

    for s in range(slots):
        w_copy(s).start()

    barrier = pltpu.get_barrier_semaphore()
    partners = [where(p, peer_of(c, k), d) for k in range(1, tensors)]
    partners += [where(pp, peer_of(c, k), d) for pp in (after, before) for k in range(tensors)]
    partners += [
        where(p, peer_of(c, k), lax.rem(d + e, dps)) for e in range(1, dps) for k in range(tensors)
    ]
    for partner in partners:
        pl.semaphore_signal(
            barrier, inc=1, device_id=partner, device_id_type=pl.DeviceIdType.MESH
        )
    pl.semaphore_wait(barrier, len(partners))

    def row_ds(cc):
        return pl.ds(pl.multiple_of(cc * rows, rows), rows)

    def col_ds(cc):
        return pl.ds(pl.multiple_of(cc * quarter, quarter), quarter)

    def cut_ds(cc, r):
        return pl.ds(pl.multiple_of(cc * quarter + r * cut, cut), cut)

    def span(r):
        return slice(r * cut, (r + 1) * cut)

    def opening_src(src, buf, q, cc):
        m, t = q // splits, q % splits
        part = src.at[m, t * rows : (t + 1) * rows]
        return part if buf is hbuf else part.at[:, col_ds(cc)]

    def opening(src, buf, q, k):
        return remote(
            opening_src(src, buf, q, peer_of(c, k)),
            buf.at[q, row_ds(c)],
            in_send.at[q, k - 1],
            in_recv.at[q, k - 1],
            where(p, peer_of(c, k), d),
        )

    def opening_own(src, buf, q):
        return pltpu.make_async_copy(
            opening_src(src, buf, q, c), buf.at[q, row_ds(c)], own_sem.at[q]
        )

    def opening_all(src, buf):
        for q in range(chunks):
            for k in (2, 3, 1):
                opening(src, buf, q, k).start()
        for q in range(chunks):
            opening_own(src, buf, q).start()

    def opening_wait(src, buf, q):
        whole = src.at[0, 0:rows]
        for k in range(1, tensors):
            part = whole if buf is hbuf else whole.at[:, col_ds(c)]
            remote(
                part,
                buf.at[q, row_ds(c)],
                in_send.at[q, k - 1],
                in_recv.at[q, k - 1],
                where(p, peer_of(c, k), d),
            ).wait_recv()
        part = whole if buf is hbuf else whole.at[:, col_ds(c)]
        pltpu.make_async_copy(part, buf.at[q, row_ds(c)], own_sem.at[q]).wait()

    @pl.when(p == 0)
    def _():
        opening_all(x_ref, hbuf)

    @pl.when(p >= pipes - 2)
    def _():
        opening_all(cot_ref, dcol)

    def to_dp(item, slot, q, k):
        return remote(
            normed.at[item],
            h_out.at[slot, d, q],
            dp_send.at[item, k - 1],
            dp_recv.at[item, k - 1],
            where(p, c, lax.rem(d + k, dps)),
        )

    def to_own(item, slot, q):
        return pltpu.make_async_copy(normed.at[item], h_out.at[slot, d, q], loc_sem.at[0, item])

    def h_shares(item, slot, q):
        to_own(item, slot, q).start()
        for k in range(1, dps):
            to_dp(item, slot, q, k).start()

    def d_own(item, slot, q):
        return pltpu.make_async_copy(
            dcol.at[item], d_all.at[slot, d, q, :, col_ds(c)], loc_sem.at[1, item]
        )

    def d_share(item, slot, q, e, k):
        return remote(
            dcol.at[item],
            d_all.at[slot, d, q, :, col_ds(c)],
            dg_send.at[item, e, k],
            dg_recv.at[item, e, k],
            where(p, peer_of(c, k), lax.rem(d + e, dps)),
        )

    far_shares = [(e, k) for e in range(dps - 1, -1, -1) for k in (2, 0) if e or k]

    def d_shares(item, slot, q):
        return [d_share(item, slot, q, e, k) for e, k in far_shares + [(0, 1)]]

    def d_shares_all(first, slot):
        for q in range(chunks):
            for share in d_shares(first + q, slot, q):
                share.start()
            d_own(first + q, slot, q).start()

    def d_relay(item, slot, q, e, k, arriving=False):
        origin = peer_of(peer_of(c, 1), k) if arriving else peer_of(c, k)
        ref = d_all.at[slot, lax.rem(d + dps - e, dps), q, :, col_ds(origin)]
        return remote(
            ref, ref, dr_send.at[item, e, k], dr_recv.at[item, e, k], where(p, peer_of(c, 1), d)
        )

    def d_relays(item, slot, q):
        for e, k in far_shares:
            d_share(item, slot, q, e, k).wait_recv()
            d_relay(item, slot, q, e, k).start()

    def d_flush(item, slot, q):
        return pltpu.make_async_copy(
            d_all.at[slot, :, q], d_out.at[slot, :, q], loc_sem.at[2, item]
        )

    def d_gather(item, slot, q):
        d_own(item, slot, q).wait()
        for e, k in far_shares:
            d_relay(item, slot, q, e, k, True).wait_recv()
        d_share(item, slot, q, 0, 1).wait_recv()
        d_flush(item, slot, q).start()

    def f_along(item, target_item, k, r):
        return remote(
            nxt.at[item, :, span(r)],
            hbuf.at[target_item, :, cut_ds(c, r)],
            f1_send.at[item, k // 2, r],
            f1_recv.at[target_item, k // 2, r],
            where(after, peer_of(c, k), d),
        )

    def f_arrive(item, k, r):
        ref = hbuf.at[item, :, cut_ds(peer_of(c, k), r)]
        remote(
            ref, ref, f1_send.at[item, k // 2, r], f1_recv.at[item, k // 2, r], where(after, c, d)
        ).wait_recv()
        spread(item, k, r).start()

    def spread(item, k, r, arriving=False):
        origin = peer_of(peer_of(c, 1), k) if arriving else peer_of(c, k)
        ref = hbuf.at[item, :, cut_ds(origin, r)]
        return remote(
            ref,
            ref,
            fx_send.at[item, k // 2, r],
            fx_recv.at[item, k // 2, r],
            where(p, peer_of(c, 1), d),
        )

    def ab_copy(item, target_item, k, r):
        src, dst = (b_send, b_recv) if k else (a_send, a_recv)
        return remote(
            src.at[item, :, span(r)],
            dst.at[target_item, :, span(r)],
            ab_send.at[item, k // 2, r],
            ab_recv.at[target_item, k // 2, r],
            where(before, peer_of(c, k), d),
        )

    def far_copy(item, r):
        return remote(
            far_send.at[item, :, span(r)],
            far_recv.at[item, :, span(r)],
            s3_send.at[item, r],
            s3_recv.at[item, r],
            where(p, peer_of(c, 1), d),
        )

    def near_copy(item, r):
        return remote(
            near_send.at[item, :, span(r)],
            near_recv.at[item, :, span(r)],
            s1_send.at[item, r],
            s1_recv.at[item, r],
            where(p, peer_of(c, 1), d),
        )

    def inner_copy(item, target_item, k):
        return remote(
            isend.at[item],
            irecv.at[target_item, k],
            is_send.at[item, k],
            is_recv.at[target_item, k],
            where(before, peer_of(c, k), d),
        )

    def turn_copy(q, k):
        return remote(
            tsend.at[q],
            trecv.at[q, k - 1],
            ts_send.at[q, k - 1],
            ts_recv.at[q, k - 1],
            where(p, peer_of(c, k), d),
        )

    def flat(first, second):
        lanes = [jnp.broadcast_to(v, (group, 128)) for v in (first, second)]
        square = jnp.concatenate([lanes[i % 2] for i in range(128 // group)], axis=0)
        return jnp.transpose(square)[:8]

    def upright(sums):
        tall = jnp.transpose(jnp.concatenate([sums] * 16, axis=0))
        return tall[:group, :1], tall[group : 2 * group, :1]

    def before_item(item):
        return item + chunks * (1 - (p + pipes - 1) // pipes)

    def reduce(item, slot, stored):
        ahead = stored is None
        columns = dcol[item]
        target_item = before_item(item)
        inner = jnp.zeros((group, 1), jnp.float32)
        if not ahead:
            inverse_rms = rms[stored][:, :1]
        order = [(3, r) for r in range(cuts)] + [(1, 0)] + [(2, r) for r in range(cuts)]
        order += [(1, r) for r in range(1, cuts)] + [(0, r) for r in range(cuts)]
        for k, r in order:
            where_to = cut_ds(peer_of(c, k), r)
            gain = g_ref[slot, :, where_to]
            term = jnp.dot(columns, w_t[slot, :, where_to], preferred_element_type=jnp.float32)
            if k == 3:
                far_send[item, :, span(r)] = term.astype(jnp.bfloat16)
                far_copy(item, r).start()
            elif k == 1:
                near_send[item, :, span(r)] = term.astype(jnp.bfloat16)
                near_copy(item, r).start()
            elif k == 2:
                far_copy(item, r).wait_recv()
                both = gain * (term + far_recv[item, :, span(r)].astype(jnp.float32))
                if not ahead:
                    both = inverse_rms * both
                b_send[item, :, span(r)] = both.astype(jnp.bfloat16)
                ab_copy(item, target_item, 2, r).start()
            else:
                near_copy(item, r).wait_recv()
                both = gain * (term + near_recv[item, :, span(r)].astype(jnp.float32))
                if not ahead:
                    both = dcol[item, :, span(r)].astype(jnp.float32) + inverse_rms * both
                a_send[item, :, span(r)] = both.astype(jnp.bfloat16)
                ab_copy(item, target_item, 0, r).start()
            if not ahead:
                hidden = hbuf[stored, :, where_to].astype(jnp.float32)
                inner += jnp.sum(hidden * (gain * term), axis=-1, keepdims=True)
        if not ahead:
            factor = inverse_rms * inverse_rms * inverse_rms * (inner * (1.0 / width))
            isend[item] = flat(factor, factor)
            for k in (2, 3, 0, 1):
                inner_copy(item, target_item, k).start()

    def turn_over(s):
        side = 256

        def block(i, carry):
            part = pl.ds(pl.multiple_of(i * side, side), side)
            w_t[s, :, part] = jnp.transpose(w[s, part, :])
            return carry

        lax.fori_loop(0, width // side, block, 0)

    def turn_ahead(q, carry):
        opening_wait(cot_ref, dcol, q)
        reduce(q, slots - 1, None)
        return carry

    def step(t, carry):
        f_on = t < items
        item = jnp.minimum(t, items - 1)
        slot = item // chunks
        q = lax.rem(item, chunks)
        layer = slot * pipes + p
        target_item = item + chunks * ((p + 1) // pipes)

        @pl.when(f_on & (q == 0))
        def _():
            w_copy(slot).wait()

        @pl.when(f_on & (q == 0) & (slot == slots - 1))
        def _():
            turn_over(slots - 1)

            @pl.when(layer == layers - 1)
            def _():
                lax.fori_loop(0, chunks, turn_ahead, 0)
                d_shares_all(0, slots - 1)

            for s in range(slots - 1):
                turn_over(s)

        @pl.when(f_on & (layer == 0))
        def _():
            opening_wait(x_ref, hbuf, item)

        @pl.when(f_on & (layer > 0))
        def _():
            for r in range(cuts):
                f_arrive(item, 0, r)

        @pl.when(f_on & (layer < layers - 1))
        def _():
            def scaled_of(cc, r):
                part = hbuf[item, :, cut_ds(cc, r)].astype(jnp.float32)
                scaled = (part * g_ref[slot, :, cut_ds(cc, r)]).astype(jnp.bfloat16)
                return scaled, jnp.sum(part * part, axis=-1, keepdims=True)

            def piece(cc, r, first=False):
                scaled, square = scaled_of(cc, r)
                product = jnp.dot(
                    scaled, w[slot, cut_ds(cc, r), :], preferred_element_type=jnp.float32
                )
                if first:
                    acc[...] = product
                else:
                    acc[...] += product
                return square

            total = piece(c, 0, True)
            for r in range(1, cuts):
                total += piece(c, r)
            for r in range(cuts):

                @pl.when(layer > 0)
                def _(r=r):
                    f_arrive(item, 2, r)

                total += piece(peer_of(c, 2), r)
            for r in range(cuts):

                @pl.when(layer > 0)
                def _(r=r):
                    spread(item, 0, r, True).wait_recv()

                total += piece(peer_of(c, 1), r)
            for r in range(cuts):

                @pl.when(layer > 0)
                def _(r=r):
                    spread(item, 2, r, True).wait_recv()

                if r < cuts - 1:
                    total += piece(peer_of(c, 3), r)

            last = cut_ds(peer_of(c, 3), cuts - 1)
            scaled, square = scaled_of(peer_of(c, 3), cuts - 1)
            inverse_rms = lax.rsqrt((total + square) * (1.0 / width) + EPSILON)
            for n in range(cuts):
                product = acc[:, span(n)] + jnp.dot(
                    scaled, w[slot, last, span(n)], preferred_element_type=jnp.float32
                )
                product = (product * inverse_rms).astype(jnp.bfloat16).astype(jnp.float32)
                nxt[item, :, span(n)] = (
                    hbuf[item, :, cut_ds(c, n)].astype(jnp.float32) + product
                ).astype(jnp.bfloat16)
                f_along(item, target_item, 2, n).start()
                f_along(item, target_item, 0, n).start()
            rms[item] = jnp.broadcast_to(inverse_rms, (group, 128))

        @pl.when(f_on & (layer == layers - 2))
        def _():
            opening_wait(cot_ref, dcol, q)
            inner = jnp.zeros((group, 1), jnp.float32)
            square = jnp.zeros((group, 1), jnp.float32)
            for r in range(cuts):
                for k in (0, 2):
                    ab_copy(q, q, k, r).wait_recv()
                hidden = nxt[item, :, span(r)].astype(jnp.float32)
                back = a_recv[q, :, span(r)].astype(jnp.float32)
                back += b_recv[q, :, span(r)].astype(jnp.float32)
                inner += jnp.sum(hidden * back, axis=-1, keepdims=True)
                square += jnp.sum(hidden * hidden, axis=-1, keepdims=True)
            tsend[q] = flat(inner, square)
            for k in (2, 3, 1):
                turn_copy(q, k).start()

        @pl.when(f_on & (layer == layers - 1))
        def _():
            for r in range(cuts):
                f_arrive(item, 2, r)
            for r in range(cuts):
                spread(item, 0, r, True).wait_recv()
                spread(item, 2, r, True).wait_recv()

        b_step(t)

        for s in range(slots):
            late = jnp.where(p == pipes - 2, 1, 0) if s == slots - 1 else 0

            @pl.when(t == (s + 1) * chunks - 1 + late)
            def _(s=s):
                lax.fori_loop(s * chunks, (s + 1) * chunks, normalize, 0)

        return carry

    def normalize(item, carry):
        slot = item // chunks
        wide = hbuf[item].astype(jnp.float32)
        mean = jnp.mean(wide * wide, axis=-1, keepdims=True)
        normed[item] = (wide * lax.rsqrt(mean + EPSILON) * g_ref[slot]).astype(jnp.bfloat16)
        h_shares(item, slot, lax.rem(item, chunks))
        return carry

    def b_step(t):
        early = jnp.where(p == pipes - 2, chunks - 1, 0)
        b_time = t - (items - early)
        b_on = (b_time >= 0) & (b_time < items)
        item = jnp.clip(b_time, 0, items - 1)
        slot = slots - 1 - item // chunks
        q = lax.rem(item, chunks)
        layer = slot * pipes + p
        stored = slot * chunks + q

        @pl.when(b_on & (q == 0) & (slot < slots - 1))
        def _():
            for back in range(chunks):
                d_relays(item - chunks + back, slot + 1, back)
            for back in range(chunks):
                d_gather(item - chunks + back, slot + 1, back)

        @pl.when(b_on & (layer == layers - 2))
        def _():
            for k in range(1, tensors):
                turn_copy(q, k).wait_recv()
            sums = tsend[q]
            for k in range(1, tensors):
                sums += trecv[q, k - 1]
            inner, square = upright(sums)
            inverse_rms = lax.rsqrt(square * (1.0 / width) + EPSILON)
            factor = inverse_rms * inverse_rms * inverse_rms * (inner * (1.0 / width))
            for r in range(cuts):
                back = a_recv[item, :, span(r)].astype(jnp.float32)
                back += b_recv[item, :, span(r)].astype(jnp.float32)
                dcol[item, :, span(r)] = (
                    dcol[item, :, span(r)].astype(jnp.float32)
                    + inverse_rms * back
                    - factor * nxt[stored, :, span(r)].astype(jnp.float32)
                ).astype(jnp.bfloat16)

        @pl.when(b_on & (layer < layers - 2))
        def _():
            for k in range(tensors):
                inner_copy(item, item, k).wait_recv()
            sums = irecv[item, 0]
            for k in range(1, tensors):
                sums += irecv[item, k]
            factor, _ = upright(sums)
            for r in range(cuts):
                for k in (2, 0):
                    ab_copy(item, item, k, r).wait_recv()
                dcol[item, :, span(r)] = (
                    a_recv[item, :, span(r)].astype(jnp.float32)
                    + b_recv[item, :, span(r)].astype(jnp.float32)
                    - factor * nxt[stored, :, span(r)].astype(jnp.float32)
                ).astype(jnp.bfloat16)

        @pl.when(b_on & (layer > 0) & (layer < layers - 1))
        def _():
            reduce(item, slot, stored)

        @pl.when(b_on & (slot == 0))
        def _():
            for share in d_shares(item, slot, q):
                share.start()
            d_own(item, slot, q).start()

        @pl.when(b_on & (layer == 0) & (q > 0))
        def _():
            d_relays(item - 1, slot, q - 1)

        @pl.when(b_on & (slot > 0) & (layer < layers - 1) & (q == chunks - 1))
        def _():
            d_shares_all(item - (chunks - 1), slot)

    lax.fori_loop(0, 2 * items, step, 0)

    for q in range(chunks):
        item = (slots - 1) * chunks + q
        if q == chunks - 1:
            d_relays(item, 0, q)
        else:

            @pl.when(p > 0)
            def _(item=item, q=q):
                d_relays(item, 0, q)

    for q in range(chunks):
        d_gather((slots - 1) * chunks + q, 0, q)

    @pl.when(p == 0)
    def _():
        for q in range(chunks):
            for k in range(1, tensors):
                opening(x_ref, hbuf, q, k).wait_send()

    @pl.when(p >= pipes - 2)
    def _():
        for q in range(chunks):
            for k in range(1, tensors):
                opening(cot_ref, dcol, q, k).wait_send()

    def ending(item, carry):
        f_slot = item // chunks
        b_slot = slots - 1 - item // chunks
        q = lax.rem(item, chunks)
        f_layer = f_slot * pipes + p
        b_layer = b_slot * pipes + p

        @pl.when(f_layer > 0)
        def _():
            for k in (0, 2):
                for r in range(cuts):
                    spread(item, k, r).wait_send()

        @pl.when(f_layer < layers - 1)
        def _():
            for k in (0, 2):
                for r in range(cuts):
                    f_along(item, item, k, r).wait_send()

        @pl.when(b_layer > 0)
        def _():
            for r in range(cuts):
                for k in (0, 2):
                    ab_copy(item, item, k, r).wait_send()
                far_copy(item, r).wait_send()
                near_copy(item, r).wait_send()

        @pl.when((b_layer > 0) & (b_layer < layers - 1))
        def _():
            for k in range(tensors):
                inner_copy(item, item, k).wait_send()

        @pl.when(b_layer == layers - 2)
        def _():
            for k in range(1, tensors):
                turn_copy(q, k).wait_send()

        to_own(item, f_slot, q).wait()
        d_flush(item, b_slot, q).wait()
        for k in range(1, dps):
            to_dp(item, f_slot, q, k).wait()
        for e, k in far_shares:
            d_share(item, b_slot, q, e, k).wait_send()
            d_relay(item, b_slot, q, e, k).wait_send()
        d_share(item, b_slot, q, 0, 1).wait_send()
        return carry

    lax.fori_loop(0, items, ending, 0)


def chain(inputs, weights, norm_gains, cotangent):
    micro, own_rows, width = inputs.shape
    slots = weights.shape[0]
    quarter = weights.shape[3]
    pipes = lax.axis_size("pipe")
    tensors = lax.axis_size("tensor")
    dps = lax.axis_size("dp")
    splits = SPLITS
    cuts = CUTS
    rows = own_rows // splits
    chunks = micro * splits
    items = slots * chunks
    group = tensors * rows
    dims = (chunks, splits, slots, rows, width, quarter, pipes, tensors, dps, cuts)
    vmem = pl.BlockSpec(memory_space=pltpu.VMEM)
    hbm = pl.BlockSpec(memory_space=pl.ANY)
    dma = pltpu.SemaphoreType.DMA
    out = jax.ShapeDtypeStruct((slots, dps, chunks, group, width), jnp.bfloat16)
    piece = pltpu.VMEM((items, group, quarter), jnp.bfloat16)
    return pl.pallas_call(
        functools.partial(chain_kernel, dims),
        out_shape=(out, out),
        in_specs=[vmem, hbm, vmem, vmem],
        out_specs=(hbm, hbm),
        scratch_shapes=[
            pltpu.VMEM((slots, width, quarter), jnp.bfloat16),
            pltpu.VMEM((slots, quarter, width), jnp.bfloat16),
            pltpu.VMEM((items, group, width), jnp.bfloat16),
            pltpu.VMEM((items, group, width), jnp.bfloat16),
            piece,
            pltpu.VMEM((slots, dps, chunks, group, width), jnp.bfloat16),
            pltpu.VMEM((items, group, 128), jnp.float32),
            pltpu.VMEM((group, quarter), jnp.float32),
            piece,
            piece,
            piece,
            piece,
            piece,
            piece,
            piece,
            piece,
            piece,
            pltpu.VMEM((items, 8, 128), jnp.float32),
            pltpu.VMEM((items, tensors, 8, 128), jnp.float32),
            pltpu.VMEM((chunks, 8, 128), jnp.float32),
            pltpu.VMEM((chunks, tensors - 1, 8, 128), jnp.float32),
            dma((slots,)),
            dma((chunks,)),
            dma((chunks, tensors - 1)),
            dma((chunks, tensors - 1)),
            dma((items, 2, cuts)),
            dma((items, 2, cuts)),
            dma((items, 2, cuts)),
            dma((items, 2, cuts)),
            dma((items, 2, cuts)),
            dma((items, 2, cuts)),
            dma((items, cuts)),
            dma((items, cuts)),
            dma((items, cuts)),
            dma((items, cuts)),
            dma((items, tensors)),
            dma((items, tensors)),
            dma((chunks, tensors - 1)),
            dma((chunks, tensors - 1)),
            dma((items, dps - 1)),
            dma((items, dps - 1)),
            dma((items, dps, tensors)),
            dma((items, dps, tensors)),
            dma((items, dps, tensors)),
            dma((items, dps, tensors)),
            dma((3, items)),
        ],
        compiler_params=pltpu.CompilerParams(
            collective_id=0, has_side_effects=True, vmem_limit_bytes=62 * 1024 * 1024
        ),
        name="chain",
    )(inputs, weights, norm_gains, cotangent)


def gram_kernel(base_rows, scale, h_hbm, d_hbm, h_ref, d_ref, act_ref, grad_ref, own, lhs, sem):
    slots, tokens, span = h_ref.shape
    lanes = 128
    mixed = lanes * slots

    @pl.when(pl.program_id(0) == 0)
    def _():
        place = lax.axis_index("tensor") * lax.axis_size("dp") + lax.axis_index("dp")
        columns = pl.ds(pl.multiple_of(place * base_rows, base_rows), base_rows)
        copies = [
            pltpu.make_async_copy(source.at[:, :, columns], own.at[i], sem.at[i])
            for i, source in enumerate((h_hbm, d_hbm))
        ]
        for copy in copies:
            copy.start()
        row = lax.broadcasted_iota(jnp.int32, (mixed, lanes), 0)
        column = lax.broadcasted_iota(jnp.int32, (mixed, lanes), 1)
        for i in range(2):
            copies[i].wait()
            for s in range(slots):
                pick = jnp.where(row == column * slots + s, 1.0, 0.0).astype(jnp.bfloat16)
                for b in range(base_rows // lanes):
                    spread = lax.dot_general(
                        pick,
                        own[i, s, :, b * lanes : (b + 1) * lanes],
                        (((1,), (1,)), ((), ())),
                        preferred_element_type=jnp.float32,
                    )
                    lhs[i, b * mixed : (b + 1) * mixed, s * tokens : (s + 1) * tokens] = (
                        spread.astype(jnp.bfloat16)
                    )

    for i, (source, out) in enumerate(((h_ref, act_ref), (d_ref, grad_ref))):
        rhs = source[...].reshape(slots * tokens, span)
        for b in range(base_rows // lanes):
            gram = jnp.dot(
                lhs[i, b * mixed : (b + 1) * mixed], rhs, preferred_element_type=jnp.float32
            )
            out[b * lanes : (b + 1) * lanes] = (
                (gram * scale).astype(jnp.bfloat16).reshape(lanes, slots, span)
            )


def gram_call(h_all, d_all, own_rows):
    slots, tokens, width = h_all.shape
    span = min(SPAN, width)
    out = jax.ShapeDtypeStruct((own_rows, slots, width), jnp.bfloat16)
    whole = pl.BlockSpec(memory_space=pl.ANY)
    source = pl.BlockSpec((slots, tokens, span), lambda n: (0, 0, n))
    target = pl.BlockSpec((own_rows, slots, span), lambda n: (0, 0, n))
    outs = pl.pallas_call(
        functools.partial(gram_kernel, own_rows, 1.0 / tokens),
        grid=(width // span,),
        out_shape=(out, out),
        in_specs=[whole, whole, source, source],
        out_specs=(target, target),
        scratch_shapes=[
            pltpu.VMEM((2, slots, tokens, own_rows), jnp.bfloat16),
            pltpu.VMEM((2, own_rows * slots, slots * tokens), jnp.bfloat16),
            pltpu.SemaphoreType.DMA((2,)),
        ],
        compiler_params=pltpu.CompilerParams(vmem_limit_bytes=60 << 20),
        name="gram",
    )(h_all, d_all, h_all, d_all)
    return tuple(o.reshape(own_rows, slots, 1, width) for o in outs)


def body(inputs, weights, norm_gains, cotangent):
    micro, rows, width = inputs.shape
    slots = weights.shape[0]
    quarter = weights.shape[3]
    tensors = lax.axis_size("tensor")
    dps = lax.axis_size("dp")
    own_rows = quarter // dps
    tokens = micro * rows * tensors * dps
    h_all, d_all = chain(inputs, weights, norm_gains, cotangent)
    h_all = h_all.reshape(slots, tokens, width)
    d_all = d_all.reshape(slots, tokens, width)
    return gram_call(h_all, d_all, own_rows)


def solution(mesh):
    in_specs = (
        P(None, ("tensor", "dp"), None),
        P(None, "pipe", None, "tensor"),
        P(None, "pipe", None),
        P(None, ("tensor", "dp"), None),
    )
    out_specs = (P(("tensor", "dp"), None, "pipe", None), P(("tensor", "dp"), None, "pipe", None))
    return jax.shard_map(body, mesh=mesh, in_specs=in_specs, out_specs=out_specs, check_vma=False)
```

```python
import functools

import jax
import jax.numpy as jnp
from jax import lax
from jax.experimental import pallas as pl
from jax.experimental.pallas import tpu as pltpu
from jax.sharding import PartitionSpec as P

EPSILON = 1e-05
SPLITS = 2
CUTS = 1
TALL = 128
SPAN = 1024


def peer_of(c, k):
    return lax.rem(c // 2 + k // 2, 2) * 2 + lax.rem(c + k, 2)


def chain_kernel(
    dims,
    x_ref,
    w_hbm,
    g_ref,
    cot_ref,
    h_out,
    d_out,
    w,
    w_t,
    hbuf,
    normed,
    dcol,
    d_all,
    rms,
    acc,
    nxt,
    far_send,
    far_recv,
    near_send,
    near_recv,
    a_send,
    a_recv,
    b_send,
    b_recv,
    isend,
    irecv,
    tsend,
    trecv,
    w_sem,
    own_sem,
    in_send,
    in_recv,
    f1_send,
    f1_recv,
    fx_send,
    fx_recv,
    ab_send,
    ab_recv,
    s3_send,
    s3_recv,
    s1_send,
    s1_recv,
    is_send,
    is_recv,
    ts_send,
    ts_recv,
    dp_send,
    dp_recv,
    dg_send,
    dg_recv,
    dr_send,
    dr_recv,
    loc_sem,
):
    chunks, splits, slots, rows, width, quarter, pipes, tensors, dps, cuts = dims
    items = slots * chunks
    layers = slots * pipes
    group = tensors * rows
    cut = quarter // cuts
    p = lax.axis_index("pipe")
    c = lax.axis_index("tensor")
    d = lax.axis_index("dp")
    after = lax.rem(p + 1, pipes)
    before = lax.rem(p + pipes - 1, pipes)

    def where(pp, cc, dd):
        return {"pipe": pp, "tensor": cc, "dp": dd}

    def remote(src, dst, send, recv, target):
        return pltpu.make_async_remote_copy(
            src_ref=src,
            dst_ref=dst,
            send_sem=send,
            recv_sem=recv,
            device_id=target,
            device_id_type=pl.DeviceIdType.MESH,
        )

    def w_copy(s):
        return pltpu.make_async_copy(w_hbm.at[s, 0], w.at[s], w_sem.at[s])

    for s in range(slots):
        w_copy(s).start()

    barrier = pltpu.get_barrier_semaphore()
    partners = [where(p, peer_of(c, k), d) for k in range(1, tensors)]
    partners += [where(pp, peer_of(c, k), d) for pp in (after, before) for k in range(tensors)]
    partners += [
        where(p, peer_of(c, k), lax.rem(d + e, dps)) for e in range(1, dps) for k in range(tensors)
    ]
    for partner in partners:
        pl.semaphore_signal(
            barrier, inc=1, device_id=partner, device_id_type=pl.DeviceIdType.MESH
        )
    pl.semaphore_wait(barrier, len(partners))

    def row_ds(cc):
        return pl.ds(pl.multiple_of(cc * rows, rows), rows)

    def col_ds(cc):
        return pl.ds(pl.multiple_of(cc * quarter, quarter), quarter)

    def cut_ds(cc, r):
        return pl.ds(pl.multiple_of(cc * quarter + r * cut, cut), cut)

    def span(r):
        return slice(r * cut, (r + 1) * cut)

    def opening_src(src, buf, q, cc):
        m, t = q // splits, q % splits
        part = src.at[m, t * rows : (t + 1) * rows]
        return part if buf is hbuf else part.at[:, col_ds(cc)]

    def opening(src, buf, q, k):
        return remote(
            opening_src(src, buf, q, peer_of(c, k)),
            buf.at[q, row_ds(c)],
            in_send.at[q, k - 1],
            in_recv.at[q, k - 1],
            where(p, peer_of(c, k), d),
        )

    def opening_own(src, buf, q):
        return pltpu.make_async_copy(
            opening_src(src, buf, q, c), buf.at[q, row_ds(c)], own_sem.at[q]
        )

    def opening_all(src, buf):
        for q in range(chunks):
            for k in (2, 3, 1):
                opening(src, buf, q, k).start()
        for q in range(chunks):
            opening_own(src, buf, q).start()

    def opening_wait(src, buf, q):
        whole = src.at[0, 0:rows]
        for k in range(1, tensors):
            part = whole if buf is hbuf else whole.at[:, col_ds(c)]
            remote(
                part,
                buf.at[q, row_ds(c)],
                in_send.at[q, k - 1],
                in_recv.at[q, k - 1],
                where(p, peer_of(c, k), d),
            ).wait_recv()
        part = whole if buf is hbuf else whole.at[:, col_ds(c)]
        pltpu.make_async_copy(part, buf.at[q, row_ds(c)], own_sem.at[q]).wait()

    @pl.when(p == 0)
    def _():
        opening_all(x_ref, hbuf)

    @pl.when(p >= pipes - 2)
    def _():
        opening_all(cot_ref, dcol)

    def to_dp(item, slot, q, k):
        return remote(
            normed.at[item],
            h_out.at[slot, d, q],
            dp_send.at[item, k - 1],
            dp_recv.at[item, k - 1],
            where(p, c, lax.rem(d + k, dps)),
        )

    def to_own(item, slot, q):
        return pltpu.make_async_copy(normed.at[item], h_out.at[slot, d, q], loc_sem.at[0, item])

    def h_shares(item, slot, q):
        to_own(item, slot, q).start()
        for k in range(1, dps):
            to_dp(item, slot, q, k).start()

    def d_own(item, slot, q):
        return pltpu.make_async_copy(
            dcol.at[item], d_all.at[slot, d, q, :, col_ds(c)], loc_sem.at[1, item]
        )

    def d_share(item, slot, q, e, k):
        return remote(
            dcol.at[item],
            d_all.at[slot, d, q, :, col_ds(c)],
            dg_send.at[item, e, k],
            dg_recv.at[item, e, k],
            where(p, peer_of(c, k), lax.rem(d + e, dps)),
        )

    far_shares = [(e, k) for e in range(dps - 1, -1, -1) for k in (2, 0) if e or k]

    def d_shares(item, slot, q):
        return [d_share(item, slot, q, e, k) for e, k in far_shares + [(0, 1)]]

    def d_shares_all(first, slot):
        for q in range(chunks):
            for share in d_shares(first + q, slot, q):
                share.start()
            d_own(first + q, slot, q).start()

    def d_relay(item, slot, q, e, k, arriving=False):
        origin = peer_of(peer_of(c, 1), k) if arriving else peer_of(c, k)
        ref = d_all.at[slot, lax.rem(d + dps - e, dps), q, :, col_ds(origin)]
        return remote(
            ref, ref, dr_send.at[item, e, k], dr_recv.at[item, e, k], where(p, peer_of(c, 1), d)
        )

    def d_relays(item, slot, q):
        for e, k in reversed(far_shares):
            d_share(item, slot, q, e, k).wait_recv()
            d_relay(item, slot, q, e, k).start()

    def d_flush(item, slot, q):
        return pltpu.make_async_copy(
            d_all.at[slot, :, q], d_out.at[slot, :, q], loc_sem.at[2, item]
        )

    def d_gather(item, slot, q):
        d_own(item, slot, q).wait()
        for e, k in far_shares:
            d_relay(item, slot, q, e, k, True).wait_recv()
        d_share(item, slot, q, 0, 1).wait_recv()
        d_flush(item, slot, q).start()

    def f_along(item, target_item, k, r):
        return remote(
            nxt.at[item, :, span(r)],
            hbuf.at[target_item, :, cut_ds(c, r)],
            f1_send.at[item, k // 2, r],
            f1_recv.at[target_item, k // 2, r],
            where(after, peer_of(c, k), d),
        )

    def f_arrive(item, k, r):
        ref = hbuf.at[item, :, cut_ds(peer_of(c, k), r)]
        remote(
            ref, ref, f1_send.at[item, k // 2, r], f1_recv.at[item, k // 2, r], where(after, c, d)
        ).wait_recv()
        spread(item, k, r).start()

    def spread(item, k, r, arriving=False):
        origin = peer_of(peer_of(c, 1), k) if arriving else peer_of(c, k)
        ref = hbuf.at[item, :, cut_ds(origin, r)]
        return remote(
            ref,
            ref,
            fx_send.at[item, k // 2, r],
            fx_recv.at[item, k // 2, r],
            where(p, peer_of(c, 1), d),
        )

    def ab_copy(item, target_item, k, r):
        src, dst = (b_send, b_recv) if k else (a_send, a_recv)
        return remote(
            src.at[item, :, span(r)],
            dst.at[target_item, :, span(r)],
            ab_send.at[item, k // 2, r],
            ab_recv.at[target_item, k // 2, r],
            where(before, peer_of(c, k), d),
        )

    def far_copy(item, r):
        return remote(
            far_send.at[item, :, span(r)],
            far_recv.at[item, :, span(r)],
            s3_send.at[item, r],
            s3_recv.at[item, r],
            where(p, peer_of(c, 1), d),
        )

    def near_copy(item, r):
        return remote(
            near_send.at[item, :, span(r)],
            near_recv.at[item, :, span(r)],
            s1_send.at[item, r],
            s1_recv.at[item, r],
            where(p, peer_of(c, 1), d),
        )

    def inner_copy(item, target_item, k):
        return remote(
            isend.at[item],
            irecv.at[target_item, k],
            is_send.at[item, k],
            is_recv.at[target_item, k],
            where(before, peer_of(c, k), d),
        )

    def turn_copy(q, k):
        return remote(
            tsend.at[q],
            trecv.at[q, k - 1],
            ts_send.at[q, k - 1],
            ts_recv.at[q, k - 1],
            where(p, peer_of(c, k), d),
        )

    def flat(first, second):
        lanes = [jnp.broadcast_to(v, (group, 128)) for v in (first, second)]
        square = jnp.concatenate([lanes[i % 2] for i in range(128 // group)], axis=0)
        return jnp.transpose(square)[:8]

    def upright(sums):
        tall = jnp.transpose(jnp.concatenate([sums] * 16, axis=0))
        return tall[:group, :1], tall[group : 2 * group, :1]

    def before_item(item):
        return item + chunks * (1 - (p + pipes - 1) // pipes)

    def reduce(item, slot, stored):
        ahead = stored is None
        columns = dcol[item]
        target_item = before_item(item)
        inner = jnp.zeros((group, 1), jnp.float32)
        if not ahead:
            inverse_rms = rms[stored][:, :1]
        terms = {}
        for k in (3, 1, 2, 0):
            for r in range(cuts):
                where_to = cut_ds(peer_of(c, k), r)
                term = matmul(columns, w_t[slot, :, where_to])
                if k == 3:
                    far_send[item, :, span(r)] = term.astype(jnp.bfloat16)
                    far_copy(item, r).start()
                elif k == 1:
                    near_send[item, :, span(r)] = term.astype(jnp.bfloat16)
                    near_copy(item, r).start()
                else:
                    terms[k, r] = term
                if not ahead:
                    hidden = hbuf[stored, :, where_to].astype(jnp.float32)
                    inner += jnp.sum(
                        hidden * (g_ref[slot, :, where_to] * term), axis=-1, keepdims=True
                    )
        for r in range(cuts):
            far_copy(item, r).wait_recv()
            both = g_ref[slot, :, cut_ds(peer_of(c, 2), r)] * (
                terms[2, r] + far_recv[item, :, span(r)].astype(jnp.float32)
            )
            if not ahead:
                both = inverse_rms * both
            b_send[item, :, span(r)] = both.astype(jnp.bfloat16)
            ab_copy(item, target_item, 2, r).start()
        if not ahead:
            factor = inverse_rms * inverse_rms * inverse_rms * (inner * (1.0 / width))
            isend[item] = flat(factor, factor)
            for k in (2, 3, 0, 1):
                inner_copy(item, target_item, k).start()
        for r in range(cuts):
            near_copy(item, r).wait_recv()
            both = g_ref[slot, :, cut_ds(c, r)] * (
                terms[0, r] + near_recv[item, :, span(r)].astype(jnp.float32)
            )
            if not ahead:
                both = dcol[item, :, span(r)].astype(jnp.float32) + inverse_rms * both
            a_send[item, :, span(r)] = both.astype(jnp.bfloat16)
            ab_copy(item, target_item, 0, r).start()

    def matmul(left, right):
        tall = jnp.concatenate([left] * max(1, TALL // group), axis=0)
        return jnp.dot(tall, right, preferred_element_type=jnp.float32)[:group]

    def turn_over(s):
        side = 256

        def block(i, carry):
            part = pl.ds(pl.multiple_of(i * side, side), side)
            w_t[s, :, part] = jnp.transpose(w[s, part, :])
            return carry

        lax.fori_loop(0, width // side, block, 0)

    def turn_ahead(q, carry):
        opening_wait(cot_ref, dcol, q)
        reduce(q, slots - 1, None)
        return carry

    def step(t, carry):
        f_on = t < items
        item = jnp.minimum(t, items - 1)
        slot = item // chunks
        q = lax.rem(item, chunks)
        layer = slot * pipes + p
        target_item = item + chunks * ((p + 1) // pipes)

        @pl.when(f_on & (q == 0))
        def _():
            w_copy(slot).wait()

        @pl.when(f_on & (q == 0) & (slot == slots - 1))
        def _():
            turn_over(slots - 1)

            @pl.when(layer == layers - 1)
            def _():
                lax.fori_loop(0, chunks, turn_ahead, 0)
                d_shares_all(0, slots - 1)

            for s in range(slots - 1):
                turn_over(s)

        @pl.when(f_on & (layer == 0))
        def _():
            opening_wait(x_ref, hbuf, item)

        @pl.when(f_on & (layer > 0))
        def _():
            for r in range(cuts):
                f_arrive(item, 2, r)

        @pl.when(f_on & (layer < layers - 1))
        def _():
            def scaled_of(cc, r):
                part = hbuf[item, :, cut_ds(cc, r)].astype(jnp.float32)
                scaled = (part * g_ref[slot, :, cut_ds(cc, r)]).astype(jnp.bfloat16)
                return scaled, jnp.sum(part * part, axis=-1, keepdims=True)

            def piece(cc, r, first=False):
                scaled, square = scaled_of(cc, r)
                product = matmul(scaled, w[slot, cut_ds(cc, r), :])
                if first:
                    acc[...] = product
                else:
                    acc[...] += product
                return square

            total = piece(peer_of(c, 2), 0, True)
            for r in range(1, cuts):
                total += piece(peer_of(c, 2), r)
            for r in range(cuts):

                @pl.when(layer > 0)
                def _(r=r):
                    f_arrive(item, 0, r)

                total += piece(c, r)
            for r in range(cuts):

                @pl.when(layer > 0)
                def _(r=r):
                    spread(item, 2, r, True).wait_recv()

                total += piece(peer_of(c, 3), r)
            for r in range(cuts):

                @pl.when(layer > 0)
                def _(r=r):
                    spread(item, 0, r, True).wait_recv()

                if r < cuts - 1:
                    total += piece(peer_of(c, 1), r)

            last = cut_ds(peer_of(c, 1), cuts - 1)
            scaled, square = scaled_of(peer_of(c, 1), cuts - 1)
            inverse_rms = lax.rsqrt((total + square) * (1.0 / width) + EPSILON)
            for n in range(cuts):
                product = acc[:, span(n)] + matmul(scaled, w[slot, last, span(n)])
                product = (product * inverse_rms).astype(jnp.bfloat16).astype(jnp.float32)
                nxt[item, :, span(n)] = (
                    hbuf[item, :, cut_ds(c, n)].astype(jnp.float32) + product
                ).astype(jnp.bfloat16)
                f_along(item, target_item, 2, n).start()
                f_along(item, target_item, 0, n).start()
            rms[item] = jnp.broadcast_to(inverse_rms, (group, 128))

        @pl.when(f_on & (layer == layers - 2))
        def _():
            opening_wait(cot_ref, dcol, q)
            inner = jnp.zeros((group, 1), jnp.float32)
            square = jnp.zeros((group, 1), jnp.float32)
            for r in range(cuts):
                for k in (0, 2):
                    ab_copy(q, q, k, r).wait_recv()
                hidden = nxt[item, :, span(r)].astype(jnp.float32)
                back = a_recv[q, :, span(r)].astype(jnp.float32)
                back += b_recv[q, :, span(r)].astype(jnp.float32)
                inner += jnp.sum(hidden * back, axis=-1, keepdims=True)
                square += jnp.sum(hidden * hidden, axis=-1, keepdims=True)
            tsend[q] = flat(inner, square)
            for k in (2, 3, 1):
                turn_copy(q, k).start()

        @pl.when(f_on & (layer == layers - 1))
        def _():
            for r in range(cuts):
                f_arrive(item, 0, r)
            for r in range(cuts):
                spread(item, 0, r, True).wait_recv()
                spread(item, 2, r, True).wait_recv()

        b_step(t)

        for s in range(slots):
            late = jnp.where(p == pipes - 2, 1, 0) if s == slots - 1 else 0

            @pl.when(t == (s + 1) * chunks - 1 + late)
            def _(s=s):
                lax.fori_loop(s * chunks, (s + 1) * chunks, normalize, 0)

        return carry

    def normalize(item, carry):
        slot = item // chunks
        wide = hbuf[item].astype(jnp.float32)
        mean = jnp.mean(wide * wide, axis=-1, keepdims=True)
        normed[item] = (wide * lax.rsqrt(mean + EPSILON) * g_ref[slot]).astype(jnp.bfloat16)
        h_shares(item, slot, lax.rem(item, chunks))
        return carry

    def b_step(t):
        early = jnp.where(p == pipes - 2, chunks - 1, 0)
        b_time = t - (items - early)
        b_on = (b_time >= 0) & (b_time < items)
        item = jnp.clip(b_time, 0, items - 1)
        slot = slots - 1 - item // chunks
        q = lax.rem(item, chunks)
        layer = slot * pipes + p
        stored = slot * chunks + q

        @pl.when(b_on & (q == 0) & (slot < slots - 1))
        def _():
            for back in range(chunks):
                d_relays(item - chunks + back, slot + 1, back)
            for back in range(chunks):
                d_gather(item - chunks + back, slot + 1, back)

        @pl.when(b_on & (layer == layers - 2))
        def _():
            for k in range(1, tensors):
                turn_copy(q, k).wait_recv()
            sums = tsend[q]
            for k in range(1, tensors):
                sums += trecv[q, k - 1]
            inner, square = upright(sums)
            inverse_rms = lax.rsqrt(square * (1.0 / width) + EPSILON)
            factor = inverse_rms * inverse_rms * inverse_rms * (inner * (1.0 / width))
            for r in range(cuts):
                back = a_recv[item, :, span(r)].astype(jnp.float32)
                back += b_recv[item, :, span(r)].astype(jnp.float32)
                dcol[item, :, span(r)] = (
                    dcol[item, :, span(r)].astype(jnp.float32)
                    + inverse_rms * back
                    - factor * nxt[stored, :, span(r)].astype(jnp.float32)
                ).astype(jnp.bfloat16)

        @pl.when(b_on & (layer < layers - 2))
        def _():
            for k in range(tensors):
                inner_copy(item, item, k).wait_recv()
            sums = irecv[item, 0]
            for k in range(1, tensors):
                sums += irecv[item, k]
            factor, _ = upright(sums)
            for r in range(cuts):
                for k in (2, 0):
                    ab_copy(item, item, k, r).wait_recv()
                dcol[item, :, span(r)] = (
                    a_recv[item, :, span(r)].astype(jnp.float32)
                    + b_recv[item, :, span(r)].astype(jnp.float32)
                    - factor * nxt[stored, :, span(r)].astype(jnp.float32)
                ).astype(jnp.bfloat16)

        @pl.when(b_on & (layer > 0) & (layer < layers - 1))
        def _():
            reduce(item, slot, stored)

        @pl.when(b_on & (slot == 0))
        def _():
            for share in d_shares(item, slot, q):
                share.start()
            d_own(item, slot, q).start()

        @pl.when(b_on & (layer == 0) & (q > 0))
        def _():
            d_relays(item - 1, slot, q - 1)

        @pl.when(b_on & (slot > 0) & (layer < layers - 1) & (q == chunks - 1))
        def _():
            d_shares_all(item - (chunks - 1), slot)

    lax.fori_loop(0, 2 * items, step, 0)

    for q in range(chunks):
        item = (slots - 1) * chunks + q
        if q == chunks - 1:
            d_relays(item, 0, q)
        else:

            @pl.when(p > 0)
            def _(item=item, q=q):
                d_relays(item, 0, q)

    for q in range(chunks):
        d_gather((slots - 1) * chunks + q, 0, q)

    @pl.when(p == 0)
    def _():
        for q in range(chunks):
            for k in range(1, tensors):
                opening(x_ref, hbuf, q, k).wait_send()

    @pl.when(p >= pipes - 2)
    def _():
        for q in range(chunks):
            for k in range(1, tensors):
                opening(cot_ref, dcol, q, k).wait_send()

    def ending(item, carry):
        f_slot = item // chunks
        b_slot = slots - 1 - item // chunks
        q = lax.rem(item, chunks)
        f_layer = f_slot * pipes + p
        b_layer = b_slot * pipes + p

        @pl.when(f_layer > 0)
        def _():
            for k in (0, 2):
                for r in range(cuts):
                    spread(item, k, r).wait_send()

        @pl.when(f_layer < layers - 1)
        def _():
            for k in (0, 2):
                for r in range(cuts):
                    f_along(item, item, k, r).wait_send()

        @pl.when(b_layer > 0)
        def _():
            for r in range(cuts):
                for k in (0, 2):
                    ab_copy(item, item, k, r).wait_send()
                far_copy(item, r).wait_send()
                near_copy(item, r).wait_send()

        @pl.when((b_layer > 0) & (b_layer < layers - 1))
        def _():
            for k in range(tensors):
                inner_copy(item, item, k).wait_send()

        @pl.when(b_layer == layers - 2)
        def _():
            for k in range(1, tensors):
                turn_copy(q, k).wait_send()

        to_own(item, f_slot, q).wait()
        d_flush(item, b_slot, q).wait()
        for k in range(1, dps):
            to_dp(item, f_slot, q, k).wait()
        for e, k in far_shares:
            d_share(item, b_slot, q, e, k).wait_send()
            d_relay(item, b_slot, q, e, k).wait_send()
        d_share(item, b_slot, q, 0, 1).wait_send()
        return carry

    lax.fori_loop(0, items, ending, 0)


def chain(inputs, weights, norm_gains, cotangent):
    micro, own_rows, width = inputs.shape
    slots = weights.shape[0]
    quarter = weights.shape[3]
    pipes = lax.axis_size("pipe")
    tensors = lax.axis_size("tensor")
    dps = lax.axis_size("dp")
    splits = SPLITS
    cuts = CUTS
    rows = own_rows // splits
    chunks = micro * splits
    items = slots * chunks
    group = tensors * rows
    dims = (chunks, splits, slots, rows, width, quarter, pipes, tensors, dps, cuts)
    vmem = pl.BlockSpec(memory_space=pltpu.VMEM)
    hbm = pl.BlockSpec(memory_space=pl.ANY)
    dma = pltpu.SemaphoreType.DMA
    out = jax.ShapeDtypeStruct((slots, dps, chunks, group, width), jnp.bfloat16)
    piece = pltpu.VMEM((items, group, quarter), jnp.bfloat16)
    return pl.pallas_call(
        functools.partial(chain_kernel, dims),
        out_shape=(out, out),
        in_specs=[vmem, hbm, vmem, vmem],
        out_specs=(hbm, hbm),
        scratch_shapes=[
            pltpu.VMEM((slots, width, quarter), jnp.bfloat16),
            pltpu.VMEM((slots, quarter, width), jnp.bfloat16),
            pltpu.VMEM((items, group, width), jnp.bfloat16),
            pltpu.VMEM((items, group, width), jnp.bfloat16),
            piece,
            pltpu.VMEM((slots, dps, chunks, group, width), jnp.bfloat16),
            pltpu.VMEM((items, group, 128), jnp.float32),
            pltpu.VMEM((group, quarter), jnp.float32),
            piece,
            piece,
            piece,
            piece,
            piece,
            piece,
            piece,
            piece,
            piece,
            pltpu.VMEM((items, 8, 128), jnp.float32),
            pltpu.VMEM((items, tensors, 8, 128), jnp.float32),
            pltpu.VMEM((chunks, 8, 128), jnp.float32),
            pltpu.VMEM((chunks, tensors - 1, 8, 128), jnp.float32),
            dma((slots,)),
            dma((chunks,)),
            dma((chunks, tensors - 1)),
            dma((chunks, tensors - 1)),
            dma((items, 2, cuts)),
            dma((items, 2, cuts)),
            dma((items, 2, cuts)),
            dma((items, 2, cuts)),
            dma((items, 2, cuts)),
            dma((items, 2, cuts)),
            dma((items, cuts)),
            dma((items, cuts)),
            dma((items, cuts)),
            dma((items, cuts)),
            dma((items, tensors)),
            dma((items, tensors)),
            dma((chunks, tensors - 1)),
            dma((chunks, tensors - 1)),
            dma((items, dps - 1)),
            dma((items, dps - 1)),
            dma((items, dps, tensors)),
            dma((items, dps, tensors)),
            dma((items, dps, tensors)),
            dma((items, dps, tensors)),
            dma((3, items)),
        ],
        compiler_params=pltpu.CompilerParams(
            collective_id=0, has_side_effects=True, vmem_limit_bytes=62 * 1024 * 1024
        ),
        name="chain",
    )(inputs, weights, norm_gains, cotangent)


def gram_kernel(base_rows, scale, h_hbm, d_hbm, h_ref, d_ref, act_ref, grad_ref, own, lhs, sem):
    slots, tokens, span = h_ref.shape
    lanes = 128
    mixed = lanes * slots

    @pl.when(pl.program_id(0) == 0)
    def _():
        place = lax.axis_index("tensor") * lax.axis_size("dp") + lax.axis_index("dp")
        columns = pl.ds(pl.multiple_of(place * base_rows, base_rows), base_rows)
        copies = [
            pltpu.make_async_copy(source.at[:, :, columns], own.at[i], sem.at[i])
            for i, source in enumerate((h_hbm, d_hbm))
        ]
        for copy in copies:
            copy.start()
        row = lax.broadcasted_iota(jnp.int32, (mixed, lanes), 0)
        column = lax.broadcasted_iota(jnp.int32, (mixed, lanes), 1)
        for i in range(2):
            copies[i].wait()
            for s in range(slots):
                pick = jnp.where(row == column * slots + s, 1.0, 0.0).astype(jnp.bfloat16)
                for b in range(base_rows // lanes):
                    spread = lax.dot_general(
                        pick,
                        own[i, s, :, b * lanes : (b + 1) * lanes],
                        (((1,), (1,)), ((), ())),
                        preferred_element_type=jnp.float32,
                    )
                    lhs[i, b * mixed : (b + 1) * mixed, s * tokens : (s + 1) * tokens] = (
                        spread.astype(jnp.bfloat16)
                    )

    for i, (source, out) in enumerate(((h_ref, act_ref), (d_ref, grad_ref))):
        rhs = source[...].reshape(slots * tokens, span)
        for b in range(base_rows // lanes):
            gram = jnp.dot(
                lhs[i, b * mixed : (b + 1) * mixed], rhs, preferred_element_type=jnp.float32
            )
            out[b * lanes : (b + 1) * lanes] = (
                (gram * scale).astype(jnp.bfloat16).reshape(lanes, slots, span)
            )


def gram_call(h_all, d_all, own_rows):
    slots, tokens, width = h_all.shape
    span = min(SPAN, width)
    out = jax.ShapeDtypeStruct((own_rows, slots, width), jnp.bfloat16)
    whole = pl.BlockSpec(memory_space=pl.ANY)
    source = pl.BlockSpec((slots, tokens, span), lambda n: (0, 0, n))
    target = pl.BlockSpec((own_rows, slots, span), lambda n: (0, 0, n))
    outs = pl.pallas_call(
        functools.partial(gram_kernel, own_rows, 1.0 / tokens),
        grid=(width // span,),
        out_shape=(out, out),
        in_specs=[whole, whole, source, source],
        out_specs=(target, target),
        scratch_shapes=[
            pltpu.VMEM((2, slots, tokens, own_rows), jnp.bfloat16),
            pltpu.VMEM((2, own_rows * slots, slots * tokens), jnp.bfloat16),
            pltpu.SemaphoreType.DMA((2,)),
        ],
        compiler_params=pltpu.CompilerParams(vmem_limit_bytes=60 << 20),
        name="gram",
    )(h_all, d_all, h_all, d_all)
    return tuple(o.reshape(own_rows, slots, 1, width) for o in outs)


def body(inputs, weights, norm_gains, cotangent):
    micro, rows, width = inputs.shape
    slots = weights.shape[0]
    quarter = weights.shape[3]
    tensors = lax.axis_size("tensor")
    dps = lax.axis_size("dp")
    own_rows = quarter // dps
    tokens = micro * rows * tensors * dps
    h_all, d_all = chain(inputs, weights, norm_gains, cotangent)
    h_all = h_all.reshape(slots, tokens, width)
    d_all = d_all.reshape(slots, tokens, width)
    return gram_call(h_all, d_all, own_rows)


def solution(mesh):
    in_specs = (
        P(None, ("tensor", "dp"), None),
        P(None, "pipe", None, "tensor"),
        P(None, "pipe", None),
        P(None, ("tensor", "dp"), None),
    )
    out_specs = (P(("tensor", "dp"), None, "pipe", None), P(("tensor", "dp"), None, "pipe", None))
    return jax.shard_map(body, mesh=mesh, in_specs=in_specs, out_specs=out_specs, check_vma=False)
```

```python
import functools

import jax
import jax.numpy as jnp
from jax import lax
from jax.experimental import pallas as pl
from jax.experimental.pallas import tpu as pltpu
from jax.sharding import PartitionSpec as P

EPSILON = 1e-05
SPLITS = 2
CUTS = 1
TALL = 128
SPAN = 1024


def peer_of(c, k):
    return lax.rem(c // 2 + k // 2, 2) * 2 + lax.rem(c + k, 2)


def chain_kernel(
    dims,
    x_ref,
    w_hbm,
    g_ref,
    cot_ref,
    h_out,
    d_out,
    w,
    w_t,
    hbuf,
    normed,
    dcol,
    d_all,
    rms,
    acc,
    nxt,
    far_send,
    far_recv,
    near_send,
    near_recv,
    a_send,
    a_recv,
    b_send,
    b_recv,
    isend,
    irecv,
    tsend,
    trecv,
    w_sem,
    own_sem,
    in_send,
    in_recv,
    f1_send,
    f1_recv,
    fx_send,
    fx_recv,
    ab_send,
    ab_recv,
    s3_send,
    s3_recv,
    s1_send,
    s1_recv,
    is_send,
    is_recv,
    ts_send,
    ts_recv,
    dp_send,
    dp_recv,
    dg_send,
    dg_recv,
    dr_send,
    dr_recv,
    loc_sem,
):
    chunks, splits, slots, rows, width, quarter, pipes, tensors, dps, cuts = dims
    items = slots * chunks
    layers = slots * pipes
    group = tensors * rows
    cut = quarter // cuts
    p = lax.axis_index("pipe")
    c = lax.axis_index("tensor")
    d = lax.axis_index("dp")
    after = lax.rem(p + 1, pipes)
    before = lax.rem(p + pipes - 1, pipes)

    def where(pp, cc, dd):
        return {"pipe": pp, "tensor": cc, "dp": dd}

    def remote(src, dst, send, recv, target):
        return pltpu.make_async_remote_copy(
            src_ref=src,
            dst_ref=dst,
            send_sem=send,
            recv_sem=recv,
            device_id=target,
            device_id_type=pl.DeviceIdType.MESH,
        )

    def w_copy(s):
        return pltpu.make_async_copy(w_hbm.at[s, 0], w.at[s], w_sem.at[s])

    w_copy(0).start()

    barrier = pltpu.get_barrier_semaphore()
    partners = [where(p, peer_of(c, k), d) for k in range(1, tensors)]
    partners += [where(pp, peer_of(c, k), d) for pp in (after, before) for k in range(tensors)]
    partners += [
        where(p, peer_of(c, k), lax.rem(d + e, dps)) for e in range(1, dps) for k in range(tensors)
    ]
    for partner in partners:
        pl.semaphore_signal(
            barrier, inc=1, device_id=partner, device_id_type=pl.DeviceIdType.MESH
        )
    pl.semaphore_wait(barrier, len(partners))

    def row_ds(cc):
        return pl.ds(pl.multiple_of(cc * rows, rows), rows)

    def col_ds(cc):
        return pl.ds(pl.multiple_of(cc * quarter, quarter), quarter)

    def cut_ds(cc, r):
        return pl.ds(pl.multiple_of(cc * quarter + r * cut, cut), cut)

    def span(r):
        return slice(r * cut, (r + 1) * cut)

    def opening_src(src, buf, q, cc):
        m, t = q // splits, q % splits
        part = src.at[m, t * rows : (t + 1) * rows]
        return part if buf is hbuf else part.at[:, col_ds(cc)]

    def opening(src, buf, q, k):
        return remote(
            opening_src(src, buf, q, peer_of(c, k)),
            buf.at[q, row_ds(c)],
            in_send.at[q, k - 1],
            in_recv.at[q, k - 1],
            where(p, peer_of(c, k), d),
        )

    def opening_own(src, buf, q):
        return pltpu.make_async_copy(
            opening_src(src, buf, q, c), buf.at[q, row_ds(c)], own_sem.at[q]
        )

    def opening_all(src, buf):
        for q in range(chunks):
            for k in (2, 3, 1):
                opening(src, buf, q, k).start()
        for q in range(chunks):
            opening_own(src, buf, q).start()

    def opening_wait(src, buf, q):
        whole = src.at[0, 0:rows]
        for k in range(1, tensors):
            part = whole if buf is hbuf else whole.at[:, col_ds(c)]
            remote(
                part,
                buf.at[q, row_ds(c)],
                in_send.at[q, k - 1],
                in_recv.at[q, k - 1],
                where(p, peer_of(c, k), d),
            ).wait_recv()
        part = whole if buf is hbuf else whole.at[:, col_ds(c)]
        pltpu.make_async_copy(part, buf.at[q, row_ds(c)], own_sem.at[q]).wait()

    @pl.when(p == 0)
    def _():
        opening_all(x_ref, hbuf)

    @pl.when(p >= pipes - 2)
    def _():
        opening_all(cot_ref, dcol)

    def to_dp(item, slot, q, k):
        return remote(
            normed.at[item],
            h_out.at[slot, d, q],
            dp_send.at[item, k - 1],
            dp_recv.at[item, k - 1],
            where(p, c, lax.rem(d + k, dps)),
        )

    def to_own(item, slot, q):
        return pltpu.make_async_copy(normed.at[item], h_out.at[slot, d, q], loc_sem.at[0, item])

    def h_shares(item, slot, q):
        to_own(item, slot, q).start()
        for k in range(1, dps):
            to_dp(item, slot, q, k).start()

    def d_own(item, slot, q):
        return pltpu.make_async_copy(
            dcol.at[item], d_all.at[slot, d, q, :, col_ds(c)], loc_sem.at[1, item]
        )

    def d_share(item, slot, q, e, k):
        return remote(
            dcol.at[item],
            d_all.at[slot, d, q, :, col_ds(c)],
            dg_send.at[item, e, k],
            dg_recv.at[item, e, k],
            where(p, peer_of(c, k), lax.rem(d + e, dps)),
        )

    far_shares = [(e, k) for e in range(dps - 1, -1, -1) for k in (2, 0) if e or k]

    def d_shares(item, slot, q):
        return [d_share(item, slot, q, e, k) for e, k in far_shares + [(0, 1)]]

    def d_shares_all(first, slot):
        for q in range(chunks):
            for share in d_shares(first + q, slot, q):
                share.start()
            d_own(first + q, slot, q).start()

    def d_relay(item, slot, q, e, k, arriving=False):
        origin = peer_of(peer_of(c, 1), k) if arriving else peer_of(c, k)
        ref = d_all.at[slot, lax.rem(d + dps - e, dps), q, :, col_ds(origin)]
        return remote(
            ref, ref, dr_send.at[item, e, k], dr_recv.at[item, e, k], where(p, peer_of(c, 1), d)
        )

    def d_relays(item, slot, q):
        for e, k in reversed(far_shares):
            d_share(item, slot, q, e, k).wait_recv()
            d_relay(item, slot, q, e, k).start()

    def d_flush(item, slot, q):
        return pltpu.make_async_copy(
            d_all.at[slot, :, q], d_out.at[slot, :, q], loc_sem.at[2, item]
        )

    def d_gather(item, slot, q):
        d_own(item, slot, q).wait()
        for e, k in far_shares:
            d_relay(item, slot, q, e, k, True).wait_recv()
        d_share(item, slot, q, 0, 1).wait_recv()
        d_flush(item, slot, q).start()

    def f_along(item, target_item, k, r):
        return remote(
            nxt.at[item, :, span(r)],
            hbuf.at[target_item, :, cut_ds(c, r)],
            f1_send.at[item, k // 2, r],
            f1_recv.at[target_item, k // 2, r],
            where(after, peer_of(c, k), d),
        )

    def f_arrive(item, k, r):
        ref = hbuf.at[item, :, cut_ds(peer_of(c, k), r)]
        remote(
            ref, ref, f1_send.at[item, k // 2, r], f1_recv.at[item, k // 2, r], where(after, c, d)
        ).wait_recv()
        spread(item, k, r).start()

    def spread(item, k, r, arriving=False):
        origin = peer_of(peer_of(c, 1), k) if arriving else peer_of(c, k)
        ref = hbuf.at[item, :, cut_ds(origin, r)]
        return remote(
            ref,
            ref,
            fx_send.at[item, k // 2, r],
            fx_recv.at[item, k // 2, r],
            where(p, peer_of(c, 1), d),
        )

    def ab_copy(item, target_item, k, r):
        src, dst = (b_send, b_recv) if k else (a_send, a_recv)
        return remote(
            src.at[item, :, span(r)],
            dst.at[target_item, :, span(r)],
            ab_send.at[item, k // 2, r],
            ab_recv.at[target_item, k // 2, r],
            where(before, peer_of(c, k), d),
        )

    def far_copy(item, r):
        return remote(
            far_send.at[item, :, span(r)],
            far_recv.at[item, :, span(r)],
            s3_send.at[item, r],
            s3_recv.at[item, r],
            where(p, peer_of(c, 1), d),
        )

    def near_copy(item, r):
        return remote(
            near_send.at[item, :, span(r)],
            near_recv.at[item, :, span(r)],
            s1_send.at[item, r],
            s1_recv.at[item, r],
            where(p, peer_of(c, 1), d),
        )

    def inner_copy(item, target_item, k):
        return remote(
            isend.at[item],
            irecv.at[target_item, k],
            is_send.at[item, k],
            is_recv.at[target_item, k],
            where(before, peer_of(c, k), d),
        )

    def turn_copy(q, k):
        return remote(
            tsend.at[q],
            trecv.at[q, k - 1],
            ts_send.at[q, k - 1],
            ts_recv.at[q, k - 1],
            where(p, peer_of(c, k), d),
        )

    def flat(first, second):
        lanes = [jnp.broadcast_to(v, (group, 128)) for v in (first, second)]
        square = jnp.concatenate([lanes[i % 2] for i in range(128 // group)], axis=0)
        return jnp.transpose(square)[:8]

    def upright(sums):
        tall = jnp.transpose(jnp.concatenate([sums] * 16, axis=0))
        return tall[:group, :1], tall[group : 2 * group, :1]

    def before_item(item):
        return item + chunks * (1 - (p + pipes - 1) // pipes)

    def reduce(item, slot, stored):
        ahead = stored is None
        columns = dcol[item]
        target_item = before_item(item)
        inner = jnp.zeros((group, 1), jnp.float32)
        if not ahead:
            inverse_rms = rms[stored][:, :1]
        terms = {}
        for k in (3, 1, 2, 0):
            for r in range(cuts):
                where_to = cut_ds(peer_of(c, k), r)
                term = matmul(columns, w_t[slot, :, where_to])
                if k == 3:
                    far_send[item, :, span(r)] = term.astype(jnp.bfloat16)
                    far_copy(item, r).start()
                elif k == 1:
                    near_send[item, :, span(r)] = term.astype(jnp.bfloat16)
                    near_copy(item, r).start()
                else:
                    terms[k, r] = term
                if not ahead:
                    hidden = hbuf[stored, :, where_to].astype(jnp.float32)
                    inner += jnp.sum(
                        hidden * (g_ref[slot, :, where_to] * term), axis=-1, keepdims=True
                    )
        for r in range(cuts):
            far_copy(item, r).wait_recv()
            both = g_ref[slot, :, cut_ds(peer_of(c, 2), r)] * (
                terms[2, r] + far_recv[item, :, span(r)].astype(jnp.float32)
            )
            if not ahead:
                both = inverse_rms * both
            b_send[item, :, span(r)] = both.astype(jnp.bfloat16)
            ab_copy(item, target_item, 2, r).start()
        if not ahead:
            factor = inverse_rms * inverse_rms * inverse_rms * (inner * (1.0 / width))
            isend[item] = flat(factor, factor)
            for k in (2, 3, 0, 1):
                inner_copy(item, target_item, k).start()
        for r in range(cuts):
            near_copy(item, r).wait_recv()
            both = g_ref[slot, :, cut_ds(c, r)] * (
                terms[0, r] + near_recv[item, :, span(r)].astype(jnp.float32)
            )
            if not ahead:
                both = dcol[item, :, span(r)].astype(jnp.float32) + inverse_rms * both
            a_send[item, :, span(r)] = both.astype(jnp.bfloat16)
            ab_copy(item, target_item, 0, r).start()

    def matmul(left, right):
        tall = jnp.concatenate([left] * max(1, TALL // group), axis=0)
        return jnp.dot(tall, right, preferred_element_type=jnp.float32)[:group]

    def turn_over(s):
        side = 256

        def block(i, carry):
            part = pl.ds(pl.multiple_of(i * side, side), side)
            w_t[s, :, part] = jnp.transpose(w[s, part, :])
            return carry

        lax.fori_loop(0, width // side, block, 0)

    def turn_ahead(q, carry):
        opening_wait(cot_ref, dcol, q)
        reduce(q, slots - 1, None)
        return carry

    def step(t, carry):
        f_on = t < items
        item = jnp.minimum(t, items - 1)
        slot = item // chunks
        q = lax.rem(item, chunks)
        layer = slot * pipes + p
        target_item = item + chunks * ((p + 1) // pipes)

        @pl.when(f_on & (q == 0))
        def _():
            w_copy(slot).wait()

        for s in range(1, slots):

            @pl.when(t == (s - 1) * chunks)
            def _(s=s):
                w_copy(s).start()

        @pl.when(f_on & (q == 0) & (slot == slots - 1))
        def _():
            turn_over(slots - 1)

            @pl.when(layer == layers - 1)
            def _():
                lax.fori_loop(0, chunks, turn_ahead, 0)
                d_shares_all(0, slots - 1)

            for s in range(slots - 1):
                turn_over(s)

        @pl.when(f_on & (layer == 0))
        def _():
            opening_wait(x_ref, hbuf, item)

        @pl.when(f_on & (layer > 0))
        def _():
            for r in range(cuts):
                f_arrive(item, 2, r)

        @pl.when(f_on & (layer < layers - 1))
        def _():
            def scaled_of(cc, r):
                part = hbuf[item, :, cut_ds(cc, r)].astype(jnp.float32)
                scaled = (part * g_ref[slot, :, cut_ds(cc, r)]).astype(jnp.bfloat16)
                return scaled, jnp.sum(part * part, axis=-1, keepdims=True)

            def piece(cc, r, first=False):
                scaled, square = scaled_of(cc, r)
                product = matmul(scaled, w[slot, cut_ds(cc, r), :])
                if first:
                    acc[...] = product
                else:
                    acc[...] += product
                return square

            total = piece(peer_of(c, 2), 0, True)
            for r in range(1, cuts):
                total += piece(peer_of(c, 2), r)
            for r in range(cuts):

                @pl.when(layer > 0)
                def _(r=r):
                    f_arrive(item, 0, r)

                total += piece(c, r)
            for r in range(cuts):

                @pl.when(layer > 0)
                def _(r=r):
                    spread(item, 2, r, True).wait_recv()

                total += piece(peer_of(c, 3), r)
            for r in range(cuts):

                @pl.when(layer > 0)
                def _(r=r):
                    spread(item, 0, r, True).wait_recv()

                if r < cuts - 1:
                    total += piece(peer_of(c, 1), r)

            last = cut_ds(peer_of(c, 1), cuts - 1)
            scaled, square = scaled_of(peer_of(c, 1), cuts - 1)
            inverse_rms = lax.rsqrt((total + square) * (1.0 / width) + EPSILON)
            for n in range(cuts):
                product = acc[:, span(n)] + matmul(scaled, w[slot, last, span(n)])
                product = (product * inverse_rms).astype(jnp.bfloat16).astype(jnp.float32)
                nxt[item, :, span(n)] = (
                    hbuf[item, :, cut_ds(c, n)].astype(jnp.float32) + product
                ).astype(jnp.bfloat16)
                f_along(item, target_item, 2, n).start()
                f_along(item, target_item, 0, n).start()
            rms[item] = jnp.broadcast_to(inverse_rms, (group, 128))

        @pl.when(f_on & (layer == layers - 2))
        def _():
            opening_wait(cot_ref, dcol, q)
            inner = jnp.zeros((group, 1), jnp.float32)
            square = jnp.zeros((group, 1), jnp.float32)
            for r in range(cuts):
                for k in (0, 2):
                    ab_copy(q, q, k, r).wait_recv()
                hidden = nxt[item, :, span(r)].astype(jnp.float32)
                back = a_recv[q, :, span(r)].astype(jnp.float32)
                back += b_recv[q, :, span(r)].astype(jnp.float32)
                inner += jnp.sum(hidden * back, axis=-1, keepdims=True)
                square += jnp.sum(hidden * hidden, axis=-1, keepdims=True)
            tsend[q] = flat(inner, square)
            for k in (2, 3, 1):
                turn_copy(q, k).start()

        @pl.when(f_on & (layer == layers - 1))
        def _():
            for r in range(cuts):
                f_arrive(item, 0, r)
            for r in range(cuts):
                spread(item, 0, r, True).wait_recv()
                spread(item, 2, r, True).wait_recv()

        b_step(t)

        for s in range(slots):
            late = jnp.where(p == pipes - 2, 1, 0) if s == slots - 1 else 0

            @pl.when(t == (s + 1) * chunks - 1 + late)
            def _(s=s):
                lax.fori_loop(s * chunks, (s + 1) * chunks, normalize, 0)

        return carry

    def normalize(item, carry):
        slot = item // chunks
        wide = hbuf[item].astype(jnp.float32)
        mean = jnp.mean(wide * wide, axis=-1, keepdims=True)
        normed[item] = (wide * lax.rsqrt(mean + EPSILON) * g_ref[slot]).astype(jnp.bfloat16)
        h_shares(item, slot, lax.rem(item, chunks))
        return carry

    def b_step(t):
        early = jnp.where(p == pipes - 2, chunks - 1, 0)
        b_time = t - (items - early)
        b_on = (b_time >= 0) & (b_time < items)
        item = jnp.clip(b_time, 0, items - 1)
        slot = slots - 1 - item // chunks
        q = lax.rem(item, chunks)
        layer = slot * pipes + p
        stored = slot * chunks + q

        @pl.when(b_on & (q == 0) & (slot < slots - 1))
        def _():
            for back in range(chunks):
                d_relays(item - chunks + back, slot + 1, back)
            for back in range(chunks):
                d_gather(item - chunks + back, slot + 1, back)

        @pl.when(b_on & (layer == layers - 2))
        def _():
            for k in range(1, tensors):
                turn_copy(q, k).wait_recv()
            sums = tsend[q]
            for k in range(1, tensors):
                sums += trecv[q, k - 1]
            inner, square = upright(sums)
            inverse_rms = lax.rsqrt(square * (1.0 / width) + EPSILON)
            factor = inverse_rms * inverse_rms * inverse_rms * (inner * (1.0 / width))
            for r in range(cuts):
                back = a_recv[item, :, span(r)].astype(jnp.float32)
                back += b_recv[item, :, span(r)].astype(jnp.float32)
                dcol[item, :, span(r)] = (
                    dcol[item, :, span(r)].astype(jnp.float32)
                    + inverse_rms * back
                    - factor * nxt[stored, :, span(r)].astype(jnp.float32)
                ).astype(jnp.bfloat16)

        @pl.when(b_on & (layer < layers - 2))
        def _():
            for k in range(tensors):
                inner_copy(item, item, k).wait_recv()
            sums = irecv[item, 0]
            for k in range(1, tensors):
                sums += irecv[item, k]
            factor, _ = upright(sums)
            for r in range(cuts):
                for k in (2, 0):
                    ab_copy(item, item, k, r).wait_recv()
                dcol[item, :, span(r)] = (
                    a_recv[item, :, span(r)].astype(jnp.float32)
                    + b_recv[item, :, span(r)].astype(jnp.float32)
                    - factor * nxt[stored, :, span(r)].astype(jnp.float32)
                ).astype(jnp.bfloat16)

        @pl.when(b_on & (layer > 0) & (layer < layers - 1))
        def _():
            reduce(item, slot, stored)

        @pl.when(b_on & (slot == 0))
        def _():
            for share in d_shares(item, slot, q):
                share.start()
            d_own(item, slot, q).start()

        @pl.when(b_on & (layer == 0) & (q > 0))
        def _():
            d_relays(item - 1, slot, q - 1)

        @pl.when(b_on & (layer == 0) & (q > 1))
        def _():
            d_gather(item - 2, slot, q - 2)

        @pl.when(b_on & (slot > 0) & (layer < layers - 1) & (q == chunks - 1))
        def _():
            d_shares_all(item - (chunks - 1), slot)

    lax.fori_loop(0, 2 * items, step, 0)

    for q in range(chunks):
        item = (slots - 1) * chunks + q
        if q == chunks - 1:
            d_relays(item, 0, q)
        else:

            @pl.when(p > 0)
            def _(item=item, q=q):
                d_relays(item, 0, q)

    for q in range(chunks):
        if q >= chunks - 2:
            d_gather((slots - 1) * chunks + q, 0, q)
        else:

            @pl.when(p > 0)
            def _(q=q):
                d_gather((slots - 1) * chunks + q, 0, q)

    @pl.when(p == 0)
    def _():
        for q in range(chunks):
            for k in range(1, tensors):
                opening(x_ref, hbuf, q, k).wait_send()

    @pl.when(p >= pipes - 2)
    def _():
        for q in range(chunks):
            for k in range(1, tensors):
                opening(cot_ref, dcol, q, k).wait_send()

    def ending(item, carry):
        f_slot = item // chunks
        b_slot = slots - 1 - item // chunks
        q = lax.rem(item, chunks)
        f_layer = f_slot * pipes + p
        b_layer = b_slot * pipes + p

        @pl.when(f_layer > 0)
        def _():
            for k in (0, 2):
                for r in range(cuts):
                    spread(item, k, r).wait_send()

        @pl.when(f_layer < layers - 1)
        def _():
            for k in (0, 2):
                for r in range(cuts):
                    f_along(item, item, k, r).wait_send()

        @pl.when(b_layer > 0)
        def _():
            for r in range(cuts):
                for k in (0, 2):
                    ab_copy(item, item, k, r).wait_send()
                far_copy(item, r).wait_send()
                near_copy(item, r).wait_send()

        @pl.when((b_layer > 0) & (b_layer < layers - 1))
        def _():
            for k in range(tensors):
                inner_copy(item, item, k).wait_send()

        @pl.when(b_layer == layers - 2)
        def _():
            for k in range(1, tensors):
                turn_copy(q, k).wait_send()

        to_own(item, f_slot, q).wait()
        d_flush(item, b_slot, q).wait()
        for k in range(1, dps):
            to_dp(item, f_slot, q, k).wait()
        for e, k in far_shares:
            d_share(item, b_slot, q, e, k).wait_send()
            d_relay(item, b_slot, q, e, k).wait_send()
        d_share(item, b_slot, q, 0, 1).wait_send()
        return carry

    lax.fori_loop(0, items, ending, 0)


def chain(inputs, weights, norm_gains, cotangent):
    micro, own_rows, width = inputs.shape
    slots = weights.shape[0]
    quarter = weights.shape[3]
    pipes = lax.axis_size("pipe")
    tensors = lax.axis_size("tensor")
    dps = lax.axis_size("dp")
    splits = SPLITS
    cuts = CUTS
    rows = own_rows // splits
    chunks = micro * splits
    items = slots * chunks
    group = tensors * rows
    dims = (chunks, splits, slots, rows, width, quarter, pipes, tensors, dps, cuts)
    vmem = pl.BlockSpec(memory_space=pltpu.VMEM)
    hbm = pl.BlockSpec(memory_space=pl.ANY)
    dma = pltpu.SemaphoreType.DMA
    out = jax.ShapeDtypeStruct((slots, dps, chunks, group, width), jnp.bfloat16)
    piece = pltpu.VMEM((items, group, quarter), jnp.bfloat16)
    return pl.pallas_call(
        functools.partial(chain_kernel, dims),
        out_shape=(out, out),
        in_specs=[vmem, hbm, vmem, vmem],
        out_specs=(hbm, hbm),
        scratch_shapes=[
            pltpu.VMEM((slots, width, quarter), jnp.bfloat16),
            pltpu.VMEM((slots, quarter, width), jnp.bfloat16),
            pltpu.VMEM((items, group, width), jnp.bfloat16),
            pltpu.VMEM((items, group, width), jnp.bfloat16),
            piece,
            pltpu.VMEM((slots, dps, chunks, group, width), jnp.bfloat16),
            pltpu.VMEM((items, group, 128), jnp.float32),
            pltpu.VMEM((group, quarter), jnp.float32),
            piece,
            piece,
            piece,
            piece,
            piece,
            piece,
            piece,
            piece,
            piece,
            pltpu.VMEM((items, 8, 128), jnp.float32),
            pltpu.VMEM((items, tensors, 8, 128), jnp.float32),
            pltpu.VMEM((chunks, 8, 128), jnp.float32),
            pltpu.VMEM((chunks, tensors - 1, 8, 128), jnp.float32),
            dma((slots,)),
            dma((chunks,)),
            dma((chunks, tensors - 1)),
            dma((chunks, tensors - 1)),
            dma((items, 2, cuts)),
            dma((items, 2, cuts)),
            dma((items, 2, cuts)),
            dma((items, 2, cuts)),
            dma((items, 2, cuts)),
            dma((items, 2, cuts)),
            dma((items, cuts)),
            dma((items, cuts)),
            dma((items, cuts)),
            dma((items, cuts)),
            dma((items, tensors)),
            dma((items, tensors)),
            dma((chunks, tensors - 1)),
            dma((chunks, tensors - 1)),
            dma((items, dps - 1)),
            dma((items, dps - 1)),
            dma((items, dps, tensors)),
            dma((items, dps, tensors)),
            dma((items, dps, tensors)),
            dma((items, dps, tensors)),
            dma((3, items)),
        ],
        compiler_params=pltpu.CompilerParams(
            collective_id=0, has_side_effects=True, vmem_limit_bytes=62 * 1024 * 1024
        ),
        name="chain",
    )(inputs, weights, norm_gains, cotangent)


def gram_kernel(base_rows, scale, h_hbm, d_hbm, h_ref, d_ref, act_ref, grad_ref, own, lhs, sem):
    slots, tokens, span = h_ref.shape
    lanes = 128
    mixed = lanes * slots

    @pl.when(pl.program_id(0) == 0)
    def _():
        place = lax.axis_index("tensor") * lax.axis_size("dp") + lax.axis_index("dp")
        columns = pl.ds(pl.multiple_of(place * base_rows, base_rows), base_rows)
        copies = [
            pltpu.make_async_copy(source.at[:, :, columns], own.at[i], sem.at[i])
            for i, source in enumerate((h_hbm, d_hbm))
        ]
        for copy in copies:
            copy.start()
        row = lax.broadcasted_iota(jnp.int32, (mixed, lanes), 0)
        column = lax.broadcasted_iota(jnp.int32, (mixed, lanes), 1)
        for i in range(2):
            copies[i].wait()
            for s in range(slots):
                pick = jnp.where(row == column * slots + s, 1.0, 0.0).astype(jnp.bfloat16)
                for b in range(base_rows // lanes):
                    spread = lax.dot_general(
                        pick,
                        own[i, s, :, b * lanes : (b + 1) * lanes],
                        (((1,), (1,)), ((), ())),
                        preferred_element_type=jnp.float32,
                    )
                    lhs[i, b * mixed : (b + 1) * mixed, s * tokens : (s + 1) * tokens] = (
                        spread.astype(jnp.bfloat16)
                    )

    for i, (source, out) in enumerate(((h_ref, act_ref), (d_ref, grad_ref))):
        rhs = source[...].reshape(slots * tokens, span)
        for b in range(base_rows // lanes):
            gram = jnp.dot(
                lhs[i, b * mixed : (b + 1) * mixed], rhs, preferred_element_type=jnp.float32
            )
            out[b * lanes : (b + 1) * lanes] = (
                (gram * scale).astype(jnp.bfloat16).reshape(lanes, slots, span)
            )


def gram_call(h_all, d_all, own_rows):
    slots, tokens, width = h_all.shape
    span = min(SPAN, width)
    out = jax.ShapeDtypeStruct((own_rows, slots, width), jnp.bfloat16)
    whole = pl.BlockSpec(memory_space=pl.ANY)
    source = pl.BlockSpec((slots, tokens, span), lambda n: (0, 0, n))
    target = pl.BlockSpec((own_rows, slots, span), lambda n: (0, 0, n))
    outs = pl.pallas_call(
        functools.partial(gram_kernel, own_rows, 1.0 / tokens),
        grid=(width // span,),
        out_shape=(out, out),
        in_specs=[whole, whole, source, source],
        out_specs=(target, target),
        scratch_shapes=[
            pltpu.VMEM((2, slots, tokens, own_rows), jnp.bfloat16),
            pltpu.VMEM((2, own_rows * slots, slots * tokens), jnp.bfloat16),
            pltpu.SemaphoreType.DMA((2,)),
        ],
        compiler_params=pltpu.CompilerParams(vmem_limit_bytes=60 << 20),
        name="gram",
    )(h_all, d_all, h_all, d_all)
    return tuple(o.reshape(own_rows, slots, 1, width) for o in outs)


def body(inputs, weights, norm_gains, cotangent):
    micro, rows, width = inputs.shape
    slots = weights.shape[0]
    quarter = weights.shape[3]
    tensors = lax.axis_size("tensor")
    dps = lax.axis_size("dp")
    own_rows = quarter // dps
    tokens = micro * rows * tensors * dps
    h_all, d_all = chain(inputs, weights, norm_gains, cotangent)
    h_all = h_all.reshape(slots, tokens, width)
    d_all = d_all.reshape(slots, tokens, width)
    return gram_call(h_all, d_all, own_rows)


def solution(mesh):
    in_specs = (
        P(None, ("tensor", "dp"), None),
        P(None, "pipe", None, "tensor"),
        P(None, "pipe", None),
        P(None, ("tensor", "dp"), None),
    )
    out_specs = (P(("tensor", "dp"), None, "pipe", None), P(("tensor", "dp"), None, "pipe", None))
    return jax.shard_map(body, mesh=mesh, in_specs=in_specs, out_specs=out_specs, check_vma=False)
```
